256 devices in a mesh: depth: 4 (over z_hi), gx: 16 (over z_lo, y, core), gy: 4 (over x).
Axes of the slice: x: 4, y: 4, z: 8 (z_hi: 4, z_lo: 2; z = z_hi * 2 + z_lo), core: 2. Of those that a mesh axis runs over, the one named last changes fastest.
Arguments:
- source: float32 [8, 2, 4, 1024, 512], P('depth', None, None, 'gx', 'gy'), may hold values from -6 to 6
- observed: float32 [8, 2, 4, 1024, 512], P('depth', None, None, 'gx', 'gy'), may hold values from -8 to 8
- wavenumber: float32 [8, 1024, 512], P('depth', 'gx', 'gy'), may hold values from 0.5 to 1.5
- damping: float32 [8, 1024, 512], P('depth', 'gx', 'gy'), may hold values from 0.5 to 2
Outputs:
- forward_field: float32 [8, 2, 4, 1024, 512], P('depth', None, None, 'gx', 'gy')
- gradient: float32 [8, 1024, 512], P('depth', 'gx', 'gy')
The draws below stay inside these ranges and needn't reach their ends.
All inputs are finite; a program needn't handle non-finite values.
Results may differ from the reference program's by a relative error of at most 0.00002.
Values sent between devices are 32-bit elements; how exact they have to be, the bound alone decides.
A program may use at most 64 MiB of HBM per device.

```python
import math
import jax
import jax.numpy as jnp
from jax import lax

SHOTS = 4
NX = 1024
NY = 512
NZ = 8


def level_of(rng, dims, split, least, top_value):
    level, own = 1.0, jax.random.fold_in(rng, 6)
    for axis_at, shards_of in split:
        steps = jnp.exp(jax.random.uniform(jax.random.fold_in(own, axis_at), (shards_of,), jnp.float32, least / len(split), top_value / len(split)))
        level = level * jnp.repeat(steps, dims[axis_at] // shards_of).reshape([-1 if axis == axis_at else 1 for axis in range(len(dims))])
    return level


def gaussian(key, shape, width, limit, pieces=(), held_as=jnp.bfloat16):
    drawn = jax.random.normal(key, shape, jnp.float32) * width
    if len(pieces) > 0:
        drawn = level_of(key, shape, pieces, -0.22, 0.18) * drawn
    return jnp.clip(drawn, min=-limit, max=limit).astype(held_as)


def setup_inputs(seed: int = 0) -> dict:
    streams_of = jax.random.split(jax.random.key(seed), 5)
    return {
        "source": gaussian(streams_of[0], (NZ, 2, SHOTS, NX, NY), 1.0, 6.0, ((0, 4), (3, 16), (4, 4)), jnp.float32),
        "observed": gaussian(streams_of[1], (NZ, 2, SHOTS, NX, NY), 2.0, 8.0, ((0, 4), (3, 16), (4, 4)), jnp.float32),
        "wavenumber": jnp.clip(0.5 + 1.0 * jax.random.uniform(streams_of[2], (NZ, NX, NY), jnp.float32) ** level_of(streams_of[2], (NZ, NX, NY), ((0, 4), (1, 16), (2, 4)), -0.2, 0.2), 0.5, 1.5),
        "damping": jnp.clip(jnp.exp(math.log(2.0) - 1.3862944 * jax.random.uniform(streams_of[3], (NZ, NX, NY), jnp.float32) ** level_of(streams_of[3], (NZ, NX, NY), ((0, 4), (1, 16), (2, 4)), -0.2, 0.2)), 0.5, 2.0),
    }


def lateral_sum(plane):
    padded = jnp.pad(plane, ((0, 0), (0, 0), (1, 1), (1, 1)))
    return padded[:, :, 2:, 1:-1] + padded[:, :, :-2, 1:-1] + padded[:, :, 1:-1, 2:] + padded[:, :, 1:-1, :-2]


def complex_scale(plane, inverse):
    real_part = inverse[0][None]
    imag_part = inverse[1][None]
    return jnp.stack([plane[0] * real_part - plane[1] * imag_part, plane[0] * imag_part + plane[1] * real_part])


def relax(drive, inverse):
    field = complex_scale(drive, inverse)
    for sweep_step in range(2):
        field = complex_scale(drive + lateral_sum(field), inverse)
    return field


def inverses(wavenumber, damping):
    real_diag = 6.0 - wavenumber
    denom = real_diag * real_diag + damping * damping
    return real_diag / denom, damping / denom


def sweep(drive, inverse, reverse):
    def advance(carry, items):
        plane, inv_plane = items
        result = relax(plane + 2.5 * carry, inv_plane)
        return result, result

    start = jnp.zeros(drive.shape[1:], jnp.float32)
    final, fields = lax.scan(advance, start, (drive, inverse), reverse=reverse)
    return fields


def reference(source, observed, wavenumber, damping):
    inv_real, inv_imag = inverses(wavenumber, damping)
    inv_fwd = jnp.stack([inv_real, -inv_imag], axis=1)
    inv_adj = jnp.stack([inv_real, inv_imag], axis=1)
    forward_field = sweep(source, inv_fwd, False)
    residual = forward_field - observed
    adjoint = sweep(residual, inv_adj, True)
    product = forward_field[:, 0] * adjoint[:, 0] + forward_field[:, 1] * adjoint[:, 1]
    gradient = jnp.mean(product, axis=1)
    return forward_field, gradient
```

```python
import functools

import jax
import jax.numpy as jnp
from jax import lax
from jax.experimental import pallas as pl
from jax.experimental.pallas import tpu as pltpu
from jax.sharding import PartitionSpec as P

MESH = pl.DeviceIdType.MESH
CHUNK = 16
PAD = 8
LANES = 128


def kernel(
    sizes,
    planes,
    halo,
    src,
    obs,
    wavenumber,
    damping,
    fout,
    gout,
    drive,
    cols,
    cols_out,
    observed,
    resid,
    rcols,
    rcols_out,
    field,
    inv_side,
    u0,
    u1,
    u2,
    held,
    prod,
    parts,
    in_send,
    in_recv,
    obs_send,
    obs_recv,
    out_send,
    out_recv,
    grad_send,
    grad_recv,
    row_send,
    row_recv,
    col_send,
    col_recv,
    rrow_send,
    rrow_recv,
    rcol_send,
    rcol_recv,
):
    ndepth, ngx, ngy = sizes
    d = lax.axis_index("depth")
    a = lax.axis_index("gx")
    b = lax.axis_index("gy")
    depth = ndepth * planes
    rows = wavenumber.shape[1]
    ext = rows + 2 * halo
    block = pl.ds(halo, rows)
    mine = pl.ds(planes * d, planes)
    slot = 2 * halo

    up, down = lax.rem(a + ngx - 1, ngx), lax.rem(a + 1, ngx)
    left, right = lax.rem(b + ngy - 1, ngy), lax.rem(b + 1, ngy)
    sideways = [
        {"gx": x, "gy": y}
        for x, y in (
            (up, b),
            (down, b),
            (a, left),
            (a, right),
            (up, left),
            (up, right),
            (down, left),
            (down, right),
        )
    ]
    others = [lax.rem(d + i, ndepth) for i in range(1, ndepth)]
    anyone = {"depth": others[0]}

    def remote(source, target, send, recv, device):
        return pltpu.make_async_remote_copy(
            src_ref=source,
            dst_ref=target,
            send_sem=send,
            recv_sem=recv,
            device_id=device,
            device_id_type=MESH,
        )

    own_source = pltpu.make_async_copy(
        src.at[:, :, d], drive.at[mine, 0:2, block], in_recv.at[d]
    )
    own_source.start()
    pltpu.make_async_copy(obs.at[:, :, d], observed.at[mine], obs_recv.at[d]).start()

    barrier = pltpu.get_barrier_semaphore()
    for device in sideways + [{"depth": e} for e in others]:
        pl.semaphore_signal(barrier, inc=1, device_id=device, device_id_type=MESH)

    for p in range(planes):
        real_diag = 6.0 - wavenumber[p]
        damp = damping[p]
        denom = real_diag * real_diag + damp * damp
        drive[planes * d + p, 2, halo : halo + rows] = real_diag / denom
        drive[planes * d + p, 3, halo : halo + rows] = -damp / denom
    for u in (u0, u1, u2):
        u[...] = jnp.zeros_like(u)

    pl.semaphore_wait(barrier, len(sideways) + len(others))

    for i, e in enumerate(others):
        remote(
            src.at[:, :, e], drive.at[mine, 0:2, block], in_send.at[0, i], in_recv.at[d], {"depth": e}
        ).start()
        remote(
            drive.at[mine, 2:4, block],
            drive.at[mine, 2:4, block],
            in_send.at[1, i],
            in_recv.at[d],
            {"depth": e},
        ).start()

    lane = lax.broadcasted_iota(jnp.int32, (rows, LANES), 1)

    def exchange(z, whole, packed, arrived, rsend, rrecv, csend, crecv):
        top, bottom = pl.ds(halo, halo), pl.ds(rows, halo)
        above, below = pl.ds(0, halo), pl.ds(halo + rows, halo)
        first, last = pl.ds(0, halo), pl.ds(rows - halo, halo)
        for device, source, target in (
            (sideways[0], top, below),
            (sideways[1], bottom, above),
        ):
            remote(
                whole.at[z, :, source], whole.at[z, :, target], rsend.at[z], rrecv.at[z], device
            ).start()
        for device, source, side, target in (
            (sideways[2], pl.ds(0, rows), 1, block),
            (sideways[3], pl.ds(0, rows), 0, block),
            (sideways[4], first, 1, below),
            (sideways[5], first, 0, below),
            (sideways[6], last, 1, above),
            (sideways[7], last, 0, above),
        ):
            remote(
                packed.at[z, source],
                arrived.at[z, side, target],
                csend.at[z],
                crecv.at[z],
                device,
            ).start()

    def pack(pieces):
        out = pieces[0]
        for k in range(1, len(pieces)):
            here = (lane >= slot * k - halo) & (lane < slot * k + halo)
            out = jnp.where(here, pltpu.roll(pieces[k], slot * k, axis=1), out)
        return out

    def spread(e, carry):
        for p in range(planes):
            z = planes * e + p
            cols_out[z] = pack([drive[z, k, halo : halo + rows] for k in range(4)])
            exchange(z, drive, cols_out, cols, row_send, row_recv, col_send, col_recv)
        return carry

    own_source.wait()
    spread(d, 0)

    def gather(i, carry):
        e = lax.rem(d + i, ndepth)
        whole = drive.at[pl.ds(planes * e, planes), :, block]
        remote(whole, whole, in_send.at[0, 0], in_recv.at[e], anyone).wait_recv()
        return spread(e, carry)

    lax.fori_loop(1, ndepth, gather, 0)

    for i, e in enumerate(others):
        remote(
            obs.at[:, :, e], observed.at[mine], obs_send.at[i], obs_recv.at[d], {"depth": e}
        ).start()

    not_top = (a > 0).astype(jnp.float32)
    not_bottom = (a < ngx - 1).astype(jnp.float32)
    not_left = (b > 0).astype(jnp.float32)
    not_right = (b < ngy - 1).astype(jnp.float32)
    clane = lax.broadcasted_iota(jnp.int32, (CHUNK, LANES), 1)
    inside = jnp.where(
        clane < halo, not_right, jnp.where(clane >= LANES - halo, not_left, 0.0)
    )
    from_right = lax.rem(clane, slot) < halo
    at_first = clane == 0
    at_last = clane == LANES - 1
    chunks = range(0, ext, CHUNK)

    def at(r):
        return slice(PAD + r, PAD + r + CHUNK)

    def unpack(arrived, z, r, count):
        both = jnp.where(
            from_right, arrived[z, 1, r : r + CHUNK], arrived[z, 0, r : r + CHUNK]
        )
        return [both] + [
            pltpu.roll(both, LANES - slot * k, axis=1) for k in range(1, count)
        ]

    def scale(vr, vi, qr, qi, sign):
        if sign > 0:
            return vr * qr - vi * qi, vr * qi + vi * qr
        return vr * qr + vi * qi, vi * qr - vr * qi

    def stencil(u, r):
        sums = []
        for c in range(2):
            vert = [u[c + k, PAD + r - 1 : PAD + r - 1 + CHUNK] + u[c + k, PAD + r + 1 : PAD + r + 1 + CHUNK] for k in (0, 2)]
            mid, side = u[c, at(r)], u[c + 2, at(r)]
            mid_l, mid_r = pltpu.roll(mid, 1, axis=1), pltpu.roll(mid, LANES - 1, axis=1)
            side_l, side_r = pltpu.roll(side, 1, axis=1), pltpu.roll(side, LANES - 1, axis=1)
            in_mid = vert[0] + jnp.where(at_first, side_l, mid_l) + jnp.where(at_last, side_r, mid_r)
            in_side = vert[1] + jnp.where(at_first, mid_l, side_l) + jnp.where(at_last, mid_r, side_r)
            sums.append((in_mid, in_side))
        return [sums[0][0], sums[1][0], sums[0][1], sums[1][1]]

    def inverse_at(z, r):
        span = slice(r, r + CHUNK)
        return drive[z, 2, span], drive[z, 3, span], inv_side[z, 0, span], inv_side[z, 1, span]

    def write(u, r, g, inv, sign):
        mr, mi = scale(g[0], g[1], inv[0], inv[1], sign)
        sr, si = scale(g[2], g[3], inv[2], inv[3], sign)
        for k, v in enumerate((mr, mi, sr, si)):
            u[k, at(r)] = v
        return mr, mi

    def relax(z, sign, finish):
        for source, target in ((u0, u1), (u1, u2)):
            for r in chunks:
                sums = stencil(source, r)
                g = [held[k, r : r + CHUNK] + sums[k] for k in range(4)]
                mr, mi = write(target, r, g, inverse_at(z, r), sign)
                if target is u2 and halo <= r < halo + rows:
                    finish(slice(r - halo, r - halo + CHUNK), mr, mi)

    def forward(z, carry):
        edge = drive.at[z, :, pl.ds(0, 2 * halo)]
        remote(edge, edge, row_send.at[z], row_recv.at[z], anyone).wait_recv()
        remote(cols.at[z], cols.at[z], col_send.at[z], col_recv.at[z], anyone).wait_recv()
        for r in chunks:
            span = slice(r, r + CHUNK)
            piece = unpack(cols, z, r, 4)
            inv = [drive[z, 2, span], drive[z, 3, span], piece[2] * inside, piece[3] * inside]
            if r < halo:
                inv = [q * not_top for q in inv]
            if r >= halo + rows:
                inv = [q * not_bottom for q in inv]
            if r < halo or r >= halo + rows:
                drive[z, 2, span] = inv[0]
                drive[z, 3, span] = inv[1]
            inv_side[z, 0, span] = inv[2]
            inv_side[z, 1, span] = inv[3]
            base = [drive[z, 0, span], drive[z, 1, span], piece[0], piece[1]]
            g = [base[k] + 2.5 * u2[k, at(r)] for k in range(4)]
            for k in range(4):
                held[k, span] = g[k]
            write(u0, r, g, inv, 1)

        def finish(span, mr, mi):
            field[z, 0, span] = mr
            field[z, 1, span] = mi

        relax(z, 1, finish)
        return carry

    lax.fori_loop(0, depth, forward, 0)
    u2[...] = jnp.zeros_like(u2)

    def remain(i, carry):
        e = ndepth - 1 - i
        pair = observed.at[pl.ds(planes * e, planes)]
        remote(pair, pair, obs_send.at[0], obs_recv.at[e], anyone).wait_recv()
        for p in reversed(range(planes)):
            z = planes * e + p
            piece = []
            for c in range(2):
                value = field[z, c] - observed[z, c]
                resid[z, c, halo : halo + rows] = value
                piece.append(value)
            rcols_out[z] = pack(piece)
            exchange(z, resid, rcols_out, rcols, rrow_send, rrow_recv, rcol_send, rcol_recv)
        return carry

    lax.fori_loop(0, ndepth, remain, 0)

    for i, e in enumerate(others):
        theirs = pl.ds(planes * e, planes)
        remote(
            field.at[theirs], fout.at[:, :, d], out_send.at[i], out_recv.at[d], {"depth": e}
        ).start()
    pltpu.make_async_copy(field.at[mine], fout.at[:, :, d], out_recv.at[d]).start()

    def adjoint(i, carry):
        z = depth - 1 - i
        edge = resid.at[z, :, pl.ds(0, 2 * halo)]
        remote(edge, edge, rrow_send.at[z], rrow_recv.at[z], anyone).wait_recv()
        remote(rcols.at[z], rcols.at[z], rcol_send.at[z], rcol_recv.at[z], anyone).wait_recv()
        for r in chunks:
            span = slice(r, r + CHUNK)
            piece = unpack(rcols, z, r, 2)
            base = [resid[z, 0, span], resid[z, 1, span], piece[0], piece[1]]
            g = [base[k] + 2.5 * u2[k, at(r)] for k in range(4)]
            for k in range(4):
                held[k, span] = g[k]
            write(u0, r, g, inverse_at(z, r), -1)

        def finish(span, mr, mi):
            prod[z, span] = field[z, 0, span] * mr + field[z, 1, span] * mi

        relax(z, -1, finish)
        e = z // planes

        @pl.when((z == planes * e) & (e != d))
        def _():
            remote(
                prod.at[pl.ds(z, planes)], parts.at[d], grad_send.at[e], grad_recv.at[d], {"depth": e}
            ).start()

        return carry

    lax.fori_loop(0, depth, adjoint, 0)

    total = prod[mine]
    for e in others:
        remote(parts.at[e], parts.at[e], grad_send.at[e], grad_recv.at[e], anyone).wait_recv()
        total = total + parts[e]
    gout[...] = total * (1.0 / ndepth)

    for i, e in enumerate(others):
        taken = fout.at[:, :, e]
        remote(taken, taken, out_send.at[0], out_recv.at[e], anyone).wait_recv()
    taken = fout.at[:, :, d]
    pltpu.make_async_copy(field.at[mine], taken, out_recv.at[d]).wait()
    for i, e in enumerate(others):
        remote(parts.at[e], parts.at[e], grad_send.at[e], grad_recv.at[e], anyone).wait_send()
        pair = observed.at[mine]
        remote(pair, pair, obs_send.at[i], obs_recv.at[e], anyone).wait_send()
        remote(pair, pair, out_send.at[i], out_recv.at[e], anyone).wait_send()
        for k in range(2):
            remote(pair, pair, in_send.at[k, i], in_recv.at[e], anyone).wait_send()

    def finish_sends(z, carry):
        edge = drive.at[z, :, pl.ds(0, 2 * halo)]
        remote(edge, edge, row_send.at[z], row_recv.at[z], anyone).wait_send()
        remote(cols.at[z], cols.at[z], col_send.at[z], col_recv.at[z], anyone).wait_send()
        edge = resid.at[z, :, pl.ds(0, 2 * halo)]
        remote(edge, edge, rrow_send.at[z], rrow_recv.at[z], anyone).wait_send()
        remote(rcols.at[z], rcols.at[z], rcol_send.at[z], rcol_recv.at[z], anyone).wait_send()
        return carry

    lax.fori_loop(0, depth, finish_sends, 0)


def body(sizes, source, observed, wavenumber, damping):
    planes, comps, shots, rows, lanes = source.shape
    ndepth = sizes[0]
    depth = ndepth * planes
    halo = 2 * depth
    ext = rows + 2 * halo
    assert comps == 2 and shots == ndepth and lanes == LANES and 8 * halo == LANES
    vmem = lambda *shape: pltpu.VMEM(shape, jnp.float32)
    dma = lambda *shape: pltpu.SemaphoreType.DMA(shape)
    anywhere = pl.BlockSpec(memory_space=pl.ANY)
    local = pl.BlockSpec(memory_space=pltpu.VMEM)
    return pl.pallas_call(
        functools.partial(kernel, sizes, planes, halo),
        name="sweeps",
        out_shape=(
            jax.ShapeDtypeStruct(source.shape, jnp.float32),
            jax.ShapeDtypeStruct(wavenumber.shape, jnp.float32),
        ),
        in_specs=[anywhere, anywhere, local, local],
        out_specs=(anywhere, local),
        scratch_shapes=[
            vmem(depth, 4, ext, lanes),
            vmem(depth, 2, ext, lanes),
            vmem(depth, rows, lanes),
            vmem(depth, 2, rows, lanes),
            vmem(depth, 2, ext, lanes),
            vmem(depth, 2, ext, lanes),
            vmem(depth, rows, lanes),
            vmem(depth, 2, rows, lanes),
            vmem(depth, 2, ext, lanes),
            vmem(4, ext + 2 * PAD, lanes),
            vmem(4, ext + 2 * PAD, lanes),
            vmem(4, ext + 2 * PAD, lanes),
            vmem(4, ext, lanes),
            vmem(depth, rows, lanes),
            vmem(ndepth, planes, rows, lanes),
            dma(2, ndepth),
            dma(ndepth),
            dma(ndepth),
            dma(ndepth),
            dma(ndepth),
            dma(ndepth),
            dma(ndepth),
            dma(ndepth),
            dma(depth),
            dma(depth),
            dma(depth),
            dma(depth),
            dma(depth),
            dma(depth),
            dma(depth),
            dma(depth),
        ],
        compiler_params=pltpu.CompilerParams(
            collective_id=0, has_side_effects=True, vmem_limit_bytes=32 << 20
        ),
    )(source, observed, wavenumber, damping)


def solution(mesh):
    sizes = tuple(mesh.shape[axis] for axis in ("depth", "gx", "gy"))
    return jax.shard_map(
        functools.partial(body, sizes),
        mesh=mesh,
        in_specs=(
            P("depth", None, None, "gx", "gy"),
            P("depth", None, None, "gx", "gy"),
            P("depth", "gx", "gy"),
            P("depth", "gx", "gy"),
        ),
        out_specs=(P("depth", None, None, "gx", "gy"), P("depth", "gx", "gy")),
        check_vma=False,
    )
```

```python
import functools

import jax
import jax.numpy as jnp
from jax import lax
from jax.experimental import pallas as pl
from jax.experimental.pallas import tpu as pltpu
from jax.sharding import PartitionSpec as P

MESH = pl.DeviceIdType.MESH
CHUNK = 16
PAD = 8
LANES = 128
TILE = 8


def kernel(
    sizes,
    halo,
    edge,
    src,
    obs,
    wavenumber,
    damping,
    fout,
    gout,
    data,
    sides,
    folded,
    observed,
    weight,
    carry,
    carry_side,
    leave,
    leave_side,
    result,
    u0,
    u1,
    u2,
    held,
    total,
    other,
    load,
    row_send,
    row_recv,
    side_send,
    side_recv,
    carry_send,
    carry_recv,
    cside_send,
    cside_recv,
    in_send,
    in_recv,
    obs_send,
    obs_recv,
    out_send,
    out_recv,
    grad_send,
    grad_recv,
):
    ndepth, ngx, ngy = sizes
    d = lax.axis_index("depth")
    a = lax.axis_index("gx")
    b = lax.axis_index("gy")
    planes, _, shots, rows, _ = src.shape
    ext = rows + 2 * halo
    block = pl.ds(halo, rows)
    half = lax.rem(d, 2)
    lower = d // 2
    mine = 2 * lax.rem(d + lower, 2)
    theirs = 2 - mine

    def source_group(s, h):
        return 2 * s + h

    def residual_group(s, h):
        return 4 + 2 * s + h

    def inverse_group(h):
        return 8 + h

    up, down = lax.rem(a + ngx - 1, ngx), lax.rem(a + 1, ngx)
    left, right = lax.rem(b + ngy - 1, ngy), lax.rem(b + 1, ngy)
    beside = [
        {"gx": x, "gy": y}
        for x, y in (
            (up, b),
            (down, b),
            (a, left),
            (a, right),
            (up, left),
            (up, right),
            (down, left),
            (down, right),
        )
    ]
    partner = {"depth": d + 1 - 2 * half}
    through = [{"depth": ndepth - 1 - d, "gy": y} for y in (b, left, right)]
    anyone = beside[0]

    def remote(source, target, send, recv, device):
        return pltpu.make_async_remote_copy(
            src_ref=source,
            dst_ref=target,
            send_sem=send,
            recv_sem=recv,
            device_id=device,
            device_id_type=MESH,
        )

    inverse_loads = [
        pltpu.make_async_copy(wavenumber, held.at[0:planes, 0:rows], load.at[0]),
        pltpu.make_async_copy(damping, held.at[planes : 2 * planes, 0:rows], load.at[1]),
    ]
    source_loads, observed_loads = [], []
    for s in range(2):
        for p in range(planes):
            k = 2 + 4 * s + 2 * p
            pair = pl.ds(2 * p, 2)
            source_loads.append(
                pltpu.make_async_copy(
                    src.at[p, :, mine + s], data.at[source_group(s, half), pair, block], load.at[k]
                )
            )
            observed_loads.append(
                pltpu.make_async_copy(
                    obs.at[p, :, mine + s], observed.at[s, half, pair], load.at[k + 1]
                )
            )
    for copy in inverse_loads + source_loads + observed_loads:
        copy.start()

    carry[...] = jnp.zeros_like(carry)
    carry_side[...] = jnp.zeros_like(carry_side)

    barrier = pltpu.get_barrier_semaphore()
    partners = beside + [partner] + through
    for device in partners:
        pl.semaphore_signal(barrier, inc=1, device_id=device, device_id_type=MESH)

    for copy in inverse_loads:
        copy.wait()
    for p in range(planes):
        real_diag = 6.0 - held[p, 0:rows]
        damp = held[planes + p, 0:rows]
        denom = real_diag * real_diag + damp * damp
        data[inverse_group(half), 2 * p, halo : halo + rows] = real_diag / denom
        data[inverse_group(half), 2 * p + 1, halo : halo + rows] = -damp / denom

    pl.semaphore_wait(barrier, len(partners))

    own_inverse = data.at[inverse_group(half), :, block]
    remote(own_inverse, own_inverse, in_send.at[0], in_recv.at[0], partner).start()
    for s in range(2):
        for p in range(planes):
            remote(
                src.at[p, :, theirs + s],
                data.at[source_group(s, half), pl.ds(2 * p, 2), block],
                in_send.at[1 + s],
                in_recv.at[1 + s],
                partner,
            ).start()

    for u in (u0, u1):
        u[...] = jnp.zeros_like(u)
    for k in range(4):
        u2[k, 0:PAD] = jnp.zeros_like(u2[k, 0:PAD])
        u2[k, PAD + ext : 2 * PAD + ext] = jnp.zeros_like(u2[k, 0:PAD])
    total[...] = jnp.zeros_like(total)

    lane = lax.broadcasted_iota(jnp.int32, (TILE, LANES), 1)
    lane_group = lane // edge
    groups = LANES // edge

    def fold(read, count, tiles):
        for_left = for_right = None
        for k in range(tiles):
            for j in range(count):
                at = k * count + j
                moved = pltpu.roll(read(j, k), (edge * (at + 1)) % LANES, axis=1)
                if for_left is None:
                    for_left = for_right = moved
                else:
                    for_left = jnp.where(lane_group == (at + 1) % groups, moved, for_left)
                    for_right = jnp.where(lane_group == at, moved, for_right)
        return for_left, for_right

    def unfold(from_left, from_right, at):
        shift = (LANES - edge * (at + 1)) % LANES
        return jnp.where(
            lane < LANES // 2,
            pltpu.roll(from_right, shift, axis=1),
            pltpu.roll(from_left, shift, axis=1),
        )

    def exchange(g):
        for device, source, target in (
            (beside[0], pl.ds(halo, halo), pl.ds(halo + rows, halo)),
            (beside[1], pl.ds(rows, halo), pl.ds(0, halo)),
        ):
            remote(
                data.at[g, :, source], data.at[g, :, target], row_send.at[g], row_recv.at[g], device
            ).start()
        for p in range(planes):
            for_left, for_right = fold(
                lambda c, k: data[g, 2 * p + c, halo + TILE * k : halo + TILE * k + TILE], 2, rows // TILE
            )
            folded[g, 0, p] = for_left
            folded[g, 1, p] = for_right
        for device, source, side, piece in (
            (beside[2], 0, 1, 1),
            (beside[3], 1, 0, 1),
            (beside[4], 0, 1, 2),
            (beside[5], 1, 0, 2),
            (beside[6], 0, 1, 0),
            (beside[7], 1, 0, 0),
        ):
            remote(
                folded.at[g, source], sides.at[g, side, piece], side_send.at[g], side_recv.at[g], device
            ).start()

    def edges(g):
        return data.at[g, :, pl.ds(0, 2 * halo)]

    def arrive(g):
        remote(edges(g), edges(g), row_send.at[g], row_recv.at[g], anyone).wait_recv()
        remote(sides.at[g], sides.at[g], side_send.at[g], side_recv.at[g], anyone).wait_recv()

    def side_of(g, p, c, t):
        spare = halo // TILE
        inner = rows // TILE
        if t < spare:
            piece, k = 0, t + inner - spare
        elif t < spare + inner:
            piece, k = 1, t - spare
        else:
            piece, k = 2, t - spare - inner
        return unfold(sides[g, 0, piece, p], sides[g, 1, piece, p], 2 * k + c)

    exchange(inverse_group(half))
    for copy in source_loads:
        copy.wait()

    def landed(k, g):
        whole = data.at[g, :, block]
        remote(whole, whole, in_send.at[k], in_recv.at[k], anyone).wait_recv()
        exchange(g)

    def spread(i, c):
        @pl.when(i < 2)
        def _():
            exchange(source_group(i, half))

        @pl.when(i >= 2)
        def _():
            landed(i - 2, jnp.where(i == 2, inverse_group(1 - half), source_group(i - 3, 1 - half)))

        return c

    lax.fori_loop(0, 5, spread, 0)
    for s in range(2):
        for p in range(planes):
            remote(
                obs.at[p, :, theirs + s],
                observed.at[s, half, pl.ds(2 * p, 2)],
                obs_send.at[s],
                obs_recv.at[s],
                partner,
            ).start()

    not_top = (a > 0).astype(jnp.float32)
    not_bottom = (a < ngx - 1).astype(jnp.float32)
    not_left = (b > 0).astype(jnp.float32)
    not_right = (b < ngy - 1).astype(jnp.float32)
    inside = jnp.where(lane < edge, not_right, jnp.where(lane >= LANES - edge, not_left, 0.0))

    def weigh(h, carried):
        g = inverse_group(h)
        arrive(g)
        for p in range(planes):
            z = planes * h + p
            for t in range(ext // TILE):
                span = slice(TILE * t, TILE * t + TILE)
                for c in range(2):
                    mid = data[g, 2 * p + c, span]
                    side = side_of(g, p, c, t) * inside
                    if TILE * t < halo:
                        mid, side = mid * not_top, side * not_top
                    if TILE * t >= halo + rows:
                        mid, side = mid * not_bottom, side * not_bottom
                    weight[0, z, c, span] = mid
                    weight[0, z, 2 + c, span] = side
                    weight[1, z, c, span] = -mid if c else mid
                    weight[1, z, 2 + c, span] = -side if c else side
        return carried

    lax.fori_loop(0, 2, weigh, 0)
    for copy in observed_loads:
        copy.wait()

    clane = lax.broadcasted_iota(jnp.int32, (CHUNK, LANES), 1)
    at_first = clane == 0
    at_last = clane == LANES - 1
    chunks = range(0, ext, CHUNK)

    def at(r):
        return slice(PAD + r, PAD + r + CHUNK)

    def stencil(u, r):
        sums = []
        higher, lower_rows = slice(PAD + r - 1, PAD + r - 1 + CHUNK), slice(PAD + r + 1, PAD + r + 1 + CHUNK)
        for c in range(2):
            mid, side = u[c, at(r)], u[c + 2, at(r)]
            mid_l, mid_r = pltpu.roll(mid, 1, axis=1), pltpu.roll(mid, LANES - 1, axis=1)
            side_l, side_r = pltpu.roll(side, 1, axis=1), pltpu.roll(side, LANES - 1, axis=1)
            in_mid = jnp.where(at_first, side_l, mid_l) + jnp.where(at_last, side_r, mid_r)
            in_side = jnp.where(at_first, mid_l, side_l) + jnp.where(at_last, mid_r, side_r)
            sums.append(
                (
                    in_mid + (u[c, higher] + u[c, lower_rows]),
                    in_side + (u[c + 2, higher] + u[c + 2, lower_rows]),
                )
            )
        return [sums[0][0], sums[1][0], sums[0][1], sums[1][1]]

    def scaled(g, kind, z, r):
        q = [weight[kind, z, k, r : r + CHUNK] for k in range(4)]
        out = []
        for k in (0, 2):
            out.append(g[k] * q[k] - g[k + 1] * q[k + 1])
            out.append(g[k] * q[k + 1] + g[k + 1] * q[k])
        return out

    def relax(kind, s, z):
        for r in chunks:
            v = scaled([held[k, r : r + CHUNK] for k in range(4)], kind, z, r)
            for k in range(4):
                u0[k, at(r)] = v[k]
        for source, target in ((u0, u1), (u1, u2)):
            for r in chunks:
                sums = stencil(source, r)
                v = scaled([held[k, r : r + CHUNK] + sums[k] for k in range(4)], kind, z, r)
                for k in range(4):
                    target[k, at(r)] = v[k]
                if target is u2 and halo <= r < halo + rows:
                    result[kind, s, z, 0, r - halo : r - halo + CHUNK] = v[0]
                    result[kind, s, z, 1, r - halo : r - halo + CHUNK] = v[1]

    most = pl.ds(TILE, ext - 2 * TILE)

    def wait_carry(kind, s):
        @pl.when(kind != lower)
        def _():
            ref = carry_side.at[kind, s]
            remote(ref, ref, cside_send.at[kind, s], cside_recv.at[kind, s], anyone).wait_recv()
            ref = carry.at[kind, s, :, most]
            remote(ref, ref, carry_send.at[kind, s], carry_recv.at[kind, s], anyone).wait_recv()

    def hand_on(kind, s):
        for c in range(2):
            for t in range(ext // TILE):
                leave[kind, s, c, TILE * t : TILE * t + TILE] = u2[c, PAD + TILE * t : PAD + TILE * t + TILE]
            for_left, for_right = fold(
                lambda j, k: u2[c, PAD + TILE * k : PAD + TILE * k + TILE], 1, ext // TILE
            )
            leave_side[kind, s, 0, c] = for_left
            leave_side[kind, s, 1, c] = for_right

        @pl.when(kind == lower)
        def _():
            for source, device in ((0, through[1]), (1, through[2])):
                remote(
                    leave_side.at[kind, s, source],
                    carry_side.at[kind, s, 1 - source],
                    cside_send.at[kind, s],
                    cside_recv.at[kind, s],
                    device,
                ).start()
            remote(
                leave.at[kind, s, :, most],
                carry.at[kind, s, :, most],
                carry_send.at[kind, s],
                carry_recv.at[kind, s],
                through[0],
            ).start()

    def field_out(s, send):
        mine_now = result.at[0, s, pl.ds(planes * (1 - half), planes)]
        return remote(mine_now, fout.at[:, :, mine + s], out_send.at[s], out_recv.at[s], partner)

    def step(i, carried):
        kind, s = i // 2, lax.rem(i, 2)
        for h in range(2):
            arrive(4 * kind + 2 * s + h)
        wait_carry(kind, s)
        for t in range(ext // TILE):
            span = slice(TILE * t, TILE * t + TILE)
            where = slice(PAD + TILE * t, PAD + TILE * t + TILE)
            for c in range(2):
                u2[c, where] = carry[kind, s, c, span]
                u2[2 + c, where] = unfold(carry_side[kind, s, 0, c], carry_side[kind, s, 1, c], t)

        def plane(j, inner):
            z = jnp.where(kind == 0, j, 2 * planes - 1 - j)
            h, p = z // planes, lax.rem(z, planes)
            g = 4 * kind + 2 * s + h
            for t in range(ext // TILE):
                span = slice(TILE * t, TILE * t + TILE)
                where = slice(PAD + TILE * t, PAD + TILE * t + TILE)
                for c in range(2):
                    held[c, span] = data[g, 2 * p + c, span] + 2.5 * u2[c, where]
                    held[2 + c, span] = side_of(g, p, c, t) + 2.5 * u2[2 + c, where]
            relax(kind, s, z)
            return inner

        lax.fori_loop(0, 2 * planes, plane, 0)
        hand_on(kind, s)

        @pl.when(kind == 0)
        def _():
            ref = observed.at[s, 1 - half]
            remote(ref, ref, obs_send.at[s], obs_recv.at[s], anyone).wait_recv()
            for h in (1, 0):
                g = residual_group(s, h)
                for p in range(planes):
                    for c in range(2):
                        data[g, 2 * p + c, halo : halo + rows] = (
                            result[0, s, planes * h + p, c] - observed[s, h, 2 * p + c]
                        )
                exchange(g)
            field_out(s, True).start()
            pltpu.make_async_copy(
                result.at[0, s, pl.ds(planes * half, planes)], fout.at[:, :, mine + s], load.at[s]
            ).start()

        @pl.when(kind == 1)
        def _():
            for z in range(2 * planes):
                value = total[z]
                for c in range(2):
                    value = value + result[0, s, z, c] * result[1, s, z, c]
                total[z] = value

        return carried

    lax.fori_loop(0, 4, step, 0)
    remote(
        total.at[pl.ds(planes * (1 - half), planes)], other, grad_send.at[0], grad_recv.at[0], partner
    ).start()

    def finish(g, carried):
        remote(edges(g), edges(g), row_send.at[g], row_recv.at[g], anyone).wait_send()
        remote(sides.at[g], sides.at[g], side_send.at[g], side_recv.at[g], anyone).wait_send()
        return carried

    lax.fori_loop(0, 10, finish, 0)
    whole = data.at[0, :, block]
    for k in range(3):
        remote(whole, whole, in_send.at[k], in_recv.at[k], anyone).wait_send()
    for s in range(2):
        ref = observed.at[s, 0]
        remote(ref, ref, obs_send.at[s], obs_recv.at[s], anyone).wait_send()
        ref = result.at[0, s, pl.ds(planes * (1 - half), planes)]
        remote(ref, ref, out_send.at[s], out_recv.at[s], anyone).wait_send()
        remote(ref, ref, out_send.at[s], out_recv.at[s], anyone).wait_recv()
        pltpu.make_async_copy(
            result.at[0, s, pl.ds(planes * half, planes)], fout.at[:, :, mine + s], load.at[s]
        ).wait()
        for kind in range(2):

            @pl.when(kind == lower)
            def _():
                side, main = leave_side.at[kind, s], leave.at[kind, s, :, most]
                remote(side, side, cside_send.at[kind, s], cside_recv.at[kind, s], anyone).wait_send()
                remote(main, main, carry_send.at[kind, s], carry_recv.at[kind, s], anyone).wait_send()

    sent = remote(other, other, grad_send.at[0], grad_recv.at[0], anyone)
    sent.wait_recv()
    held[0:planes, 0:rows] = (total[pl.ds(planes * half, planes)] + other[...]) * (1.0 / shots)
    pltpu.sync_copy(held.at[0:planes, 0:rows], gout)
    sent.wait_send()


def body(sizes, source, observed, wavenumber, damping):
    planes, comps, shots, rows, lanes = source.shape
    ndepth = sizes[0]
    edge = 4 * planes
    halo = 2 * edge
    ext = rows + 2 * halo
    assert comps == 2 and planes == 2 and shots == 4 and ndepth == 4
    assert lanes == LANES and edge * 2 * rows == TILE * LANES
    vmem = lambda *shape: pltpu.VMEM(shape, jnp.float32)
    dma = lambda *shape: pltpu.SemaphoreType.DMA(shape)
    anywhere = pl.BlockSpec(memory_space=pl.ANY)
    return pl.pallas_call(
        functools.partial(kernel, sizes, halo, edge),
        name="sweeps",
        out_shape=(
            jax.ShapeDtypeStruct(source.shape, jnp.float32),
            jax.ShapeDtypeStruct(wavenumber.shape, jnp.float32),
        ),
        in_specs=[anywhere] * 4,
        out_specs=(anywhere, anywhere),
        scratch_shapes=[
            vmem(10, 4, ext, lanes),
            vmem(10, 2, 3, 2, TILE, lanes),
            vmem(10, 2, 2, TILE, lanes),
            vmem(2, 2, 4, rows, lanes),
            vmem(2, 4, 4, ext, lanes),
            vmem(2, 2, 2, ext, lanes),
            vmem(2, 2, 2, 2, TILE, lanes),
            vmem(2, 2, 2, ext, lanes),
            vmem(2, 2, 2, 2, TILE, lanes),
            vmem(2, 2, 4, 2, rows, lanes),
            vmem(4, ext + 2 * PAD, lanes),
            vmem(4, ext + 2 * PAD, lanes),
            vmem(4, ext + 2 * PAD, lanes),
            vmem(4, ext, lanes),
            vmem(4, rows, lanes),
            vmem(2, rows, lanes),
            dma(10),
            dma(10),
            dma(10),
            dma(10),
            dma(10),
            dma(2, 2),
            dma(2, 2),
            dma(2, 2),
            dma(2, 2),
            dma(3),
            dma(3),
            dma(2),
            dma(2),
            dma(2),
            dma(2),
            dma(1),
            dma(1),
        ],
        compiler_params=pltpu.CompilerParams(
            collective_id=0, has_side_effects=True, vmem_limit_bytes=60 << 20
        ),
    )(source, observed, wavenumber, damping)


def solution(mesh):
    sizes = tuple(mesh.shape[axis] for axis in ("depth", "gx", "gy"))
    return jax.shard_map(
        functools.partial(body, sizes),
        mesh=mesh,
        in_specs=(
            P("depth", None, None, "gx", "gy"),
            P("depth", None, None, "gx", "gy"),
            P("depth", "gx", "gy"),
            P("depth", "gx", "gy"),
        ),
        out_specs=(P("depth", None, None, "gx", "gy"), P("depth", "gx", "gy")),
        check_vma=False,
    )
```

```python
import functools

import jax
import jax.numpy as jnp
from jax import lax
from jax.experimental import pallas as pl
from jax.experimental.pallas import tpu as pltpu
from jax.sharding import PartitionSpec as P

MESH = pl.DeviceIdType.MESH
CHUNK = 16
PAD = 8
LANES = 128
TILE = 8


def kernel(
    sizes,
    halo,
    edge,
    src,
    obs,
    wavenumber,
    damping,
    fout,
    gout,
    data,
    sides,
    folded,
    observed,
    weight,
    carry,
    carry_side,
    leave,
    leave_side,
    result,
    u0,
    u1,
    u2,
    held,
    total,
    other,
    load,
    row_send,
    row_recv,
    side_send,
    side_recv,
    carry_send,
    carry_recv,
    cside_send,
    cside_recv,
    in_send,
    in_recv,
    obs_send,
    obs_recv,
    out_send,
    out_recv,
    grad_send,
    grad_recv,
):
    ndepth, ngx, ngy = sizes
    d = lax.axis_index("depth")
    a = lax.axis_index("gx")
    b = lax.axis_index("gy")
    planes, _, shots, rows, _ = src.shape
    ext = rows + 2 * halo
    block = pl.ds(halo, rows)
    half = lax.rem(d, 2)
    lower = d // 2
    mine = 2 * lax.rem(d + lower, 2)
    theirs = 2 - mine

    def source_group(s, h):
        return 2 * s + h

    def residual_group(s, h):
        return 4 + 2 * s + h

    def inverse_group(h):
        return 8 + h

    up, down = lax.rem(a + ngx - 1, ngx), lax.rem(a + 1, ngx)
    left, right = lax.rem(b + ngy - 1, ngy), lax.rem(b + 1, ngy)
    beside = [
        {"gx": x, "gy": y}
        for x, y in (
            (up, b),
            (down, b),
            (a, left),
            (a, right),
            (up, left),
            (up, right),
            (down, left),
            (down, right),
        )
    ]
    partner = {"depth": d + 1 - 2 * half}
    through = [{"depth": ndepth - 1 - d, "gy": y} for y in (b, left, right)]
    anyone = beside[0]

    barrier = pltpu.get_barrier_semaphore()
    partners = beside + [partner] + through
    for device in partners:
        pl.semaphore_signal(barrier, inc=1, device_id=device, device_id_type=MESH)

    def remote(source, target, send, recv, device):
        return pltpu.make_async_remote_copy(
            src_ref=source,
            dst_ref=target,
            send_sem=send,
            recv_sem=recv,
            device_id=device,
            device_id_type=MESH,
        )

    inverse_loads = [
        pltpu.make_async_copy(wavenumber, held.at[0:planes, 0:rows], load.at[0]),
        pltpu.make_async_copy(damping, held.at[planes : 2 * planes, 0:rows], load.at[1]),
    ]
    source_loads, observed_loads = [], []
    for s in range(2):
        for p in range(planes):
            k = 2 + 4 * s + 2 * p
            pair = pl.ds(2 * p, 2)
            source_loads.append(
                pltpu.make_async_copy(
                    src.at[p, :, mine + s], data.at[source_group(s, half), pair, block], load.at[k]
                )
            )
            observed_loads.append(
                pltpu.make_async_copy(
                    obs.at[p, :, mine + s], observed.at[s, half, pair], load.at[k + 1]
                )
            )
    for copy in inverse_loads + source_loads + observed_loads:
        copy.start()

    for copy in inverse_loads:
        copy.wait()
    for p in range(planes):
        real_diag = 6.0 - held[p, 0:rows]
        damp = held[planes + p, 0:rows]
        denom = real_diag * real_diag + damp * damp
        data[inverse_group(half), 2 * p, halo : halo + rows] = real_diag / denom
        data[inverse_group(half), 2 * p + 1, halo : halo + rows] = -damp / denom

    pl.semaphore_wait(barrier, len(partners))

    own_inverse = data.at[inverse_group(half), :, block]
    remote(own_inverse, own_inverse, in_send.at[0], in_recv.at[0], partner).start()
    for s in range(2):
        for p in range(planes):
            remote(
                src.at[p, :, theirs + s],
                data.at[source_group(s, half), pl.ds(2 * p, 2), block],
                in_send.at[1 + s],
                in_recv.at[1 + s],
                partner,
            ).start()

    for u in (u0, u1):
        u[...] = jnp.zeros_like(u)
    for k in range(4):
        u2[k, 0:PAD] = jnp.zeros_like(u2[k, 0:PAD])
        u2[k, PAD + ext : 2 * PAD + ext] = jnp.zeros_like(u2[k, 0:PAD])
    total[...] = jnp.zeros_like(total)
    none = jnp.zeros((TILE, LANES), jnp.float32)
    for s in range(2):
        for c in range(2):
            for t in range(ext // TILE):
                carry[lower, s, c, TILE * t : TILE * t + TILE] = none
            carry[1 - lower, s, c, 0:TILE] = none
            carry[1 - lower, s, c, ext - TILE : ext] = none
            for side in range(2):
                carry_side[lower, s, side, c] = none

    lane = lax.broadcasted_iota(jnp.int32, (TILE, LANES), 1)
    lane_group = lane // edge
    groups = LANES // edge

    def fold(read, count, tiles):
        for_left = for_right = None
        for k in range(tiles):
            for j in range(count):
                at = k * count + j
                moved = pltpu.roll(read(j, k), (edge * (at + 1)) % LANES, axis=1)
                if for_left is None:
                    for_left = for_right = moved
                else:
                    for_left = jnp.where(lane_group == (at + 1) % groups, moved, for_left)
                    for_right = jnp.where(lane_group == at, moved, for_right)
        return for_left, for_right

    def unfold(from_left, from_right, at):
        shift = (LANES - edge * (at + 1)) % LANES
        return jnp.where(
            lane < LANES // 2,
            pltpu.roll(from_right, shift, axis=1),
            pltpu.roll(from_left, shift, axis=1),
        )

    def exchange(g):
        for device, source, target in (
            (beside[0], pl.ds(halo, halo), pl.ds(halo + rows, halo)),
            (beside[1], pl.ds(rows, halo), pl.ds(0, halo)),
        ):
            remote(
                data.at[g, :, source], data.at[g, :, target], row_send.at[g], row_recv.at[g], device
            ).start()
        for p in range(planes):
            for_left, for_right = fold(
                lambda c, k: data[g, 2 * p + c, halo + TILE * k : halo + TILE * k + TILE], 2, rows // TILE
            )
            folded[g, 0, p] = for_left
            folded[g, 1, p] = for_right
        for device, source, side, piece in (
            (beside[2], 0, 1, 1),
            (beside[3], 1, 0, 1),
            (beside[4], 0, 1, 2),
            (beside[5], 1, 0, 2),
            (beside[6], 0, 1, 0),
            (beside[7], 1, 0, 0),
        ):
            remote(
                folded.at[g, source], sides.at[g, side, piece], side_send.at[g], side_recv.at[g], device
            ).start()

    def edges(g):
        return data.at[g, :, pl.ds(0, 2 * halo)]

    def arrive(g):
        remote(edges(g), edges(g), row_send.at[g], row_recv.at[g], anyone).wait_recv()
        remote(sides.at[g], sides.at[g], side_send.at[g], side_recv.at[g], anyone).wait_recv()

    def side_of(g, p, c, t):
        spare = halo // TILE
        inner = rows // TILE
        if t < spare:
            piece, k = 0, t + inner - spare
        elif t < spare + inner:
            piece, k = 1, t - spare
        else:
            piece, k = 2, t - spare - inner
        return unfold(sides[g, 0, piece, p], sides[g, 1, piece, p], 2 * k + c)

    exchange(inverse_group(half))
    for copy in source_loads:
        copy.wait()

    def landed(k, g):
        whole = data.at[g, :, block]
        remote(whole, whole, in_send.at[k], in_recv.at[k], anyone).wait_recv()
        exchange(g)

    def send_observed():
        for s in range(2):
            for p in range(planes):
                remote(
                    obs.at[p, :, theirs + s],
                    observed.at[s, half, pl.ds(2 * p, 2)],
                    obs_send.at[s],
                    obs_recv.at[s],
                    partner,
                ).start()

    def spread(i, c):
        @pl.when(i < 2)
        def _():
            exchange(source_group(i, half))

        @pl.when(i >= 2)
        def _():
            landed(i - 2, jnp.where(i == 2, inverse_group(1 - half), source_group(i - 3, 1 - half)))

        @pl.when(i == 4)
        def _():
            send_observed()

        return c

    lax.fori_loop(0, 5, spread, 0)
    not_top = (a > 0).astype(jnp.float32)
    not_bottom = (a < ngx - 1).astype(jnp.float32)
    not_left = (b > 0).astype(jnp.float32)
    not_right = (b < ngy - 1).astype(jnp.float32)
    inside = jnp.where(lane < edge, not_right, jnp.where(lane >= LANES - edge, not_left, 0.0))

    def weigh(h, carried):
        g = inverse_group(h)
        arrive(g)
        for p in range(planes):
            z = planes * h + p
            for t in range(ext // TILE):
                span = slice(TILE * t, TILE * t + TILE)
                for c in range(2):
                    mid = data[g, 2 * p + c, span]
                    side = side_of(g, p, c, t) * inside
                    if TILE * t < halo:
                        mid, side = mid * not_top, side * not_top
                    if TILE * t >= halo + rows:
                        mid, side = mid * not_bottom, side * not_bottom
                    weight[0, z, c, span] = mid
                    weight[0, z, 2 + c, span] = side
                    weight[1, z, c, span] = -mid if c else mid
                    weight[1, z, 2 + c, span] = -side if c else side
        return carried

    lax.fori_loop(0, 2, weigh, 0)
    for copy in observed_loads:
        copy.wait()

    clane = lax.broadcasted_iota(jnp.int32, (CHUNK, LANES), 1)
    at_first = clane == 0
    at_last = clane == LANES - 1
    chunks = range(0, ext, CHUNK)

    def at(r):
        return slice(PAD + r, PAD + r + CHUNK)

    def stencil(u, r):
        sums = []
        higher, lower_rows = slice(PAD + r - 1, PAD + r - 1 + CHUNK), slice(PAD + r + 1, PAD + r + 1 + CHUNK)
        for c in range(2):
            mid, side = u[c, at(r)], u[c + 2, at(r)]
            mid_l, mid_r = pltpu.roll(mid, 1, axis=1), pltpu.roll(mid, LANES - 1, axis=1)
            side_l, side_r = pltpu.roll(side, 1, axis=1), pltpu.roll(side, LANES - 1, axis=1)
            in_mid = jnp.where(at_first, side_l, mid_l) + jnp.where(at_last, side_r, mid_r)
            in_side = jnp.where(at_first, mid_l, side_l) + jnp.where(at_last, mid_r, side_r)
            sums.append(
                (
                    in_mid + (u[c, higher] + u[c, lower_rows]),
                    in_side + (u[c + 2, higher] + u[c + 2, lower_rows]),
                )
            )
        return [sums[0][0], sums[1][0], sums[0][1], sums[1][1]]

    def scaled(g, kind, z, r):
        q = [weight[kind, z, k, r : r + CHUNK] for k in range(4)]
        out = []
        for k in (0, 2):
            out.append(g[k] * q[k] - g[k + 1] * q[k + 1])
            out.append(g[k] * q[k + 1] + g[k + 1] * q[k])
        return out

    def relax(kind, s, z):
        for r in chunks:
            v = scaled([held[k, r : r + CHUNK] for k in range(4)], kind, z, r)
            for k in range(4):
                u0[k, at(r)] = v[k]
        for source, target in ((u0, u1), (u1, u2)):
            for r in chunks:
                sums = stencil(source, r)
                v = scaled([held[k, r : r + CHUNK] + sums[k] for k in range(4)], kind, z, r)
                for k in range(4):
                    target[k, at(r)] = v[k]
                if target is u2 and halo <= r < halo + rows:
                    result[kind, s, z, 0, r - halo : r - halo + CHUNK] = v[0]
                    result[kind, s, z, 1, r - halo : r - halo + CHUNK] = v[1]

    most = pl.ds(TILE, ext - 2 * TILE)

    def wait_carry(kind, s):
        @pl.when(kind != lower)
        def _():
            ref = carry_side.at[kind, s]
            remote(ref, ref, cside_send.at[kind, s], cside_recv.at[kind, s], anyone).wait_recv()
            ref = carry.at[kind, s, :, most]
            remote(ref, ref, carry_send.at[kind, s], carry_recv.at[kind, s], anyone).wait_recv()

    def hand_on(kind, s):
        for c in range(2):
            for t in range(ext // TILE):
                leave[kind, s, c, TILE * t : TILE * t + TILE] = u2[c, PAD + TILE * t : PAD + TILE * t + TILE]
            for_left, for_right = fold(
                lambda j, k: u2[c, PAD + TILE * k : PAD + TILE * k + TILE], 1, ext // TILE
            )
            leave_side[kind, s, 0, c] = for_left
            leave_side[kind, s, 1, c] = for_right

        @pl.when(kind == lower)
        def _():
            for source, device in ((0, through[1]), (1, through[2])):
                remote(
                    leave_side.at[kind, s, source],
                    carry_side.at[kind, s, 1 - source],
                    cside_send.at[kind, s],
                    cside_recv.at[kind, s],
                    device,
                ).start()
            remote(
                leave.at[kind, s, :, most],
                carry.at[kind, s, :, most],
                carry_send.at[kind, s],
                carry_recv.at[kind, s],
                through[0],
            ).start()

    def field_out(s):
        away = result.at[0, s, pl.ds(planes * (1 - half), planes)]
        remote(away, fout.at[:, :, mine + s], out_send.at[s], out_recv.at[s], partner).start()
        here = result.at[0, s, pl.ds(planes * half, planes)]
        pltpu.make_async_copy(here, fout.at[:, :, mine + s], load.at[s]).start()

    def step(i, carried):
        kind, s = i // 2, lax.rem(i, 2)
        for h in range(2):
            arrive(4 * kind + 2 * s + h)

        @pl.when(kind == 1)
        def _():
            field_out(s)

        wait_carry(kind, s)
        for t in range(ext // TILE):
            span = slice(TILE * t, TILE * t + TILE)
            where = slice(PAD + TILE * t, PAD + TILE * t + TILE)
            for c in range(2):
                u2[c, where] = carry[kind, s, c, span]
                u2[2 + c, where] = unfold(carry_side[kind, s, 0, c], carry_side[kind, s, 1, c], t)

        def plane(j, inner):
            z = jnp.where(kind == 0, j, 2 * planes - 1 - j)
            h, p = z // planes, lax.rem(z, planes)
            g = 4 * kind + 2 * s + h
            for t in range(ext // TILE):
                span = slice(TILE * t, TILE * t + TILE)
                where = slice(PAD + TILE * t, PAD + TILE * t + TILE)
                for c in range(2):
                    held[c, span] = data[g, 2 * p + c, span] + 2.5 * u2[c, where]
                    held[2 + c, span] = side_of(g, p, c, t) + 2.5 * u2[2 + c, where]
            relax(kind, s, z)

            @pl.when(kind == 1)
            def _():
                value = total[z]
                for c in range(2):
                    value = value + result[0, s, z, c] * result[1, s, z, c]
                total[z] = value

            @pl.when((i == 3) & (h != half))
            def _():
                remote(total.at[z], other.at[p], grad_send.at[p], grad_recv.at[p], partner).start()

            return inner

        lax.fori_loop(0, 2 * planes, plane, 0)
        hand_on(kind, s)

        @pl.when(kind == 0)
        def _():
            ref = observed.at[s, 1 - half]
            remote(ref, ref, obs_send.at[s], obs_recv.at[s], anyone).wait_recv()
            for h in (1, 0):
                g = residual_group(s, h)
                for p in range(planes):
                    for c in range(2):
                        data[g, 2 * p + c, halo : halo + rows] = (
                            result[0, s, planes * h + p, c] - observed[s, h, 2 * p + c]
                        )
                exchange(g)

        return carried

    lax.fori_loop(0, 4, step, 0)

    def finish(g, carried):
        remote(edges(g), edges(g), row_send.at[g], row_recv.at[g], anyone).wait_send()
        remote(sides.at[g], sides.at[g], side_send.at[g], side_recv.at[g], anyone).wait_send()
        return carried

    lax.fori_loop(0, 10, finish, 0)
    whole = data.at[0, :, block]
    for k in range(3):
        remote(whole, whole, in_send.at[k], in_recv.at[k], anyone).wait_send()
    for s in range(2):
        ref = observed.at[s, 0]
        remote(ref, ref, obs_send.at[s], obs_recv.at[s], anyone).wait_send()
        ref = result.at[0, s, pl.ds(planes * (1 - half), planes)]
        remote(ref, ref, out_send.at[s], out_recv.at[s], anyone).wait_send()
        remote(ref, ref, out_send.at[s], out_recv.at[s], anyone).wait_recv()
        pltpu.make_async_copy(
            result.at[0, s, pl.ds(planes * half, planes)], fout.at[:, :, mine + s], load.at[s]
        ).wait()
        for kind in range(2):

            @pl.when(kind == lower)
            def _():
                side, main = leave_side.at[kind, s], leave.at[kind, s, :, most]
                remote(side, side, cside_send.at[kind, s], cside_recv.at[kind, s], anyone).wait_send()
                remote(main, main, carry_send.at[kind, s], carry_recv.at[kind, s], anyone).wait_send()

    sent = [remote(other.at[p], other.at[p], grad_send.at[p], grad_recv.at[p], anyone) for p in range(planes)]
    for copy in sent:
        copy.wait_recv()
    held[0:planes, 0:rows] = (total[pl.ds(planes * half, planes)] + other[...]) * (1.0 / shots)
    pltpu.sync_copy(held.at[0:planes, 0:rows], gout)
    for copy in sent:
        copy.wait_send()


def body(sizes, source, observed, wavenumber, damping):
    planes, comps, shots, rows, lanes = source.shape
    ndepth = sizes[0]
    edge = 4 * planes
    halo = 2 * edge
    ext = rows + 2 * halo
    assert comps == 2 and planes == 2 and shots == 4 and ndepth == 4
    assert lanes == LANES and edge * 2 * rows == TILE * LANES
    vmem = lambda *shape: pltpu.VMEM(shape, jnp.float32)
    dma = lambda *shape: pltpu.SemaphoreType.DMA(shape)
    anywhere = pl.BlockSpec(memory_space=pl.ANY)
    return pl.pallas_call(
        functools.partial(kernel, sizes, halo, edge),
        name="sweeps",
        out_shape=(
            jax.ShapeDtypeStruct(source.shape, jnp.float32),
            jax.ShapeDtypeStruct(wavenumber.shape, jnp.float32),
        ),
        in_specs=[anywhere] * 4,
        out_specs=(anywhere, anywhere),
        scratch_shapes=[
            vmem(10, 4, ext, lanes),
            vmem(10, 2, 3, 2, TILE, lanes),
            vmem(10, 2, 2, TILE, lanes),
            vmem(2, 2, 4, rows, lanes),
            vmem(2, 4, 4, ext, lanes),
            vmem(2, 2, 2, ext, lanes),
            vmem(2, 2, 2, 2, TILE, lanes),
            vmem(2, 2, 2, ext, lanes),
            vmem(2, 2, 2, 2, TILE, lanes),
            vmem(2, 2, 4, 2, rows, lanes),
            vmem(4, ext + 2 * PAD, lanes),
            vmem(4, ext + 2 * PAD, lanes),
            vmem(4, ext + 2 * PAD, lanes),
            vmem(4, ext, lanes),
            vmem(4, rows, lanes),
            vmem(2, rows, lanes),
            dma(10),
            dma(10),
            dma(10),
            dma(10),
            dma(10),
            dma(2, 2),
            dma(2, 2),
            dma(2, 2),
            dma(2, 2),
            dma(3),
            dma(3),
            dma(2),
            dma(2),
            dma(2),
            dma(2),
            dma(2),
            dma(2),
        ],
        compiler_params=pltpu.CompilerParams(
            collective_id=0, has_side_effects=True, vmem_limit_bytes=24 << 20
        ),
    )(*(pltpu.with_memory_space_constraint(x, pltpu.HBM) for x in (source, observed, wavenumber, damping)))


def solution(mesh):
    sizes = tuple(mesh.shape[axis] for axis in ("depth", "gx", "gy"))
    return jax.shard_map(
        functools.partial(body, sizes),
        mesh=mesh,
        in_specs=(
            P("depth", None, None, "gx", "gy"),
            P("depth", None, None, "gx", "gy"),
            P("depth", "gx", "gy"),
            P("depth", "gx", "gy"),
        ),
        out_specs=(P("depth", None, None, "gx", "gy"), P("depth", "gx", "gy")),
        check_vma=False,
    )
```

```python
import functools

import jax
import jax.numpy as jnp
from jax import lax
from jax.experimental import pallas as pl
from jax.experimental.pallas import tpu as pltpu
from jax.sharding import PartitionSpec as P

MESH = pl.DeviceIdType.MESH
CHUNK = 16
PAD = 8
LANES = 128
TILE = 8


def kernel(
    sizes,
    halo,
    edge,
    src,
    obs,
    wavenumber,
    damping,
    fout,
    gout,
    data,
    sides,
    folded,
    observed,
    weight,
    carry,
    carry_side,
    leave,
    leave_side,
    result,
    u0,
    u1,
    u2,
    held,
    total,
    other,
    load,
    row_send,
    row_recv,
    side_send,
    side_recv,
    carry_send,
    carry_recv,
    cside_send,
    cside_recv,
    in_send,
    in_recv,
    obs_send,
    obs_recv,
    out_send,
    out_recv,
    grad_send,
    grad_recv,
):
    ndepth, ngx, ngy = sizes
    d = lax.axis_index("depth")
    a = lax.axis_index("gx")
    b = lax.axis_index("gy")
    planes, _, shots, rows, _ = src.shape
    ext = rows + 2 * halo
    block = pl.ds(halo, rows)
    half = lax.rem(d, 2)
    lower = d // 2
    mine = 2 * lax.rem(d + lower, 2)
    theirs = 2 - mine

    def source_group(s, h):
        return 2 * s + h

    def residual_group(s, h):
        return 4 + 2 * s + h

    def inverse_group(h):
        return 8 + h

    up, down = lax.rem(a + ngx - 1, ngx), lax.rem(a + 1, ngx)
    left, right = lax.rem(b + ngy - 1, ngy), lax.rem(b + 1, ngy)
    beside = [
        {"gx": x, "gy": y}
        for x, y in (
            (up, b),
            (down, b),
            (a, left),
            (a, right),
            (up, left),
            (up, right),
            (down, left),
            (down, right),
        )
    ]
    partner = {"depth": d + 1 - 2 * half}
    through = [{"depth": ndepth - 1 - d, "gy": y} for y in (b, left, right)]
    anyone = beside[0]

    barrier = pltpu.get_barrier_semaphore()
    partners = beside + [partner] + through
    for device in partners:
        pl.semaphore_signal(barrier, inc=1, device_id=device, device_id_type=MESH)

    def remote(source, target, send, recv, device):
        return pltpu.make_async_remote_copy(
            src_ref=source,
            dst_ref=target,
            send_sem=send,
            recv_sem=recv,
            device_id=device,
            device_id_type=MESH,
        )

    inverse_loads = [
        pltpu.make_async_copy(wavenumber, held.at[0:planes, 0:rows], load.at[0]),
        pltpu.make_async_copy(damping, held.at[planes : 2 * planes, 0:rows], load.at[1]),
    ]
    source_loads, observed_loads = [], []
    for s in range(2):
        for p in range(planes):
            k = 2 + 4 * s + 2 * p
            pair = pl.ds(2 * p, 2)
            source_loads.append(
                pltpu.make_async_copy(
                    src.at[p, :, mine + s], data.at[source_group(s, half), pair, block], load.at[k]
                )
            )
            observed_loads.append(
                pltpu.make_async_copy(
                    obs.at[p, :, mine + s], observed.at[s, half, pair], load.at[k + 1]
                )
            )
    for copy in inverse_loads + source_loads + observed_loads:
        copy.start()

    for copy in inverse_loads:
        copy.wait()
    for p in range(planes):
        real_diag = 6.0 - held[p, 0:rows]
        damp = held[planes + p, 0:rows]
        denom = real_diag * real_diag + damp * damp
        data[inverse_group(half), 2 * p, halo : halo + rows] = real_diag / denom
        data[inverse_group(half), 2 * p + 1, halo : halo + rows] = -damp / denom

    pl.semaphore_wait(barrier, len(partners))

    own_inverse = data.at[inverse_group(half), :, block]
    remote(own_inverse, own_inverse, in_send.at[0], in_recv.at[0], partner).start()
    for s in range(2):
        for p in range(planes):
            remote(
                src.at[p, :, theirs + s],
                data.at[source_group(s, half), pl.ds(2 * p, 2), block],
                in_send.at[1 + s],
                in_recv.at[1 + s],
                partner,
            ).start()

    for u in (u0, u1):
        u[...] = jnp.zeros_like(u)
    for k in range(4):
        u2[k, 0:PAD] = jnp.zeros_like(u2[k, 0:PAD])
        u2[k, PAD + ext : 2 * PAD + ext] = jnp.zeros_like(u2[k, 0:PAD])
    total[...] = jnp.zeros_like(total)
    none = jnp.zeros((TILE, LANES), jnp.float32)
    for s in range(2):
        for c in range(2):
            for t in range(ext // TILE):
                carry[lower, s, c, TILE * t : TILE * t + TILE] = none
            carry[1 - lower, s, c, 0:TILE] = none
            carry[1 - lower, s, c, ext - TILE : ext] = none
            for side in range(2):
                carry_side[lower, s, side, c] = none

    lane = lax.broadcasted_iota(jnp.int32, (TILE, LANES), 1)
    lane_group = lane // edge
    groups = LANES // edge

    def fold(read, count, tiles):
        for_left = for_right = None
        for k in range(tiles):
            for j in range(count):
                at = k * count + j
                moved = pltpu.roll(read(j, k), (edge * (at + 1)) % LANES, axis=1)
                if for_left is None:
                    for_left = for_right = moved
                else:
                    for_left = jnp.where(lane_group == (at + 1) % groups, moved, for_left)
                    for_right = jnp.where(lane_group == at, moved, for_right)
        return for_left, for_right

    def unfold(from_left, from_right, at):
        shift = (LANES - edge * (at + 1)) % LANES
        return jnp.where(
            lane < LANES // 2,
            pltpu.roll(from_right, shift, axis=1),
            pltpu.roll(from_left, shift, axis=1),
        )

    def exchange(g):
        for device, source, target in (
            (beside[0], pl.ds(halo, halo), pl.ds(halo + rows, halo)),
            (beside[1], pl.ds(rows, halo), pl.ds(0, halo)),
        ):
            remote(
                data.at[g, :, source], data.at[g, :, target], row_send.at[g], row_recv.at[g], device
            ).start()
        for p in range(planes):
            for_left, for_right = fold(
                lambda c, k: data[g, 2 * p + c, halo + TILE * k : halo + TILE * k + TILE], 2, rows // TILE
            )
            folded[g, 0, p] = for_left
            folded[g, 1, p] = for_right
        for device, source, side, piece in (
            (beside[2], 0, 1, 1),
            (beside[3], 1, 0, 1),
            (beside[4], 0, 1, 2),
            (beside[5], 1, 0, 2),
            (beside[6], 0, 1, 0),
            (beside[7], 1, 0, 0),
        ):
            remote(
                folded.at[g, source], sides.at[g, side, piece], side_send.at[g], side_recv.at[g], device
            ).start()

    def edges(g):
        return data.at[g, :, pl.ds(0, 2 * halo)]

    def arrive(g):
        remote(edges(g), edges(g), row_send.at[g], row_recv.at[g], anyone).wait_recv()
        remote(sides.at[g], sides.at[g], side_send.at[g], side_recv.at[g], anyone).wait_recv()

    def side_of(g, p, c, t):
        spare = halo // TILE
        inner = rows // TILE
        if t < spare:
            piece, k = 0, t + inner - spare
        elif t < spare + inner:
            piece, k = 1, t - spare
        else:
            piece, k = 2, t - spare - inner
        return unfold(sides[g, 0, piece, p], sides[g, 1, piece, p], 2 * k + c)

    exchange(inverse_group(half))
    for copy in source_loads:
        copy.wait()

    def landed(k, g):
        whole = data.at[g, :, block]
        remote(whole, whole, in_send.at[k], in_recv.at[k], anyone).wait_recv()
        exchange(g)

    def send_observed():
        for s in range(2):
            for p in range(planes):
                remote(
                    obs.at[p, :, theirs + s],
                    observed.at[s, half, pl.ds(2 * p, 2)],
                    obs_send.at[s],
                    obs_recv.at[s],
                    partner,
                ).start()

    def spread(i, c):
        @pl.when(i < 2)
        def _():
            exchange(source_group(i, half))

        @pl.when(i >= 2)
        def _():
            landed(i - 2, jnp.where(i == 2, inverse_group(1 - half), source_group(i - 3, 1 - half)))

        @pl.when(i == 4)
        def _():
            send_observed()

        return c

    lax.fori_loop(0, 5, spread, 0)
    not_top = (a > 0).astype(jnp.float32)
    not_bottom = (a < ngx - 1).astype(jnp.float32)
    not_left = (b > 0).astype(jnp.float32)
    not_right = (b < ngy - 1).astype(jnp.float32)
    inside = jnp.where(lane < edge, not_right, jnp.where(lane >= LANES - edge, not_left, 0.0))

    def weigh(h, carried):
        g = inverse_group(h)
        arrive(g)
        for p in range(planes):
            z = planes * h + p
            for t in range(ext // TILE):
                span = slice(TILE * t, TILE * t + TILE)
                for c in range(2):
                    mid = data[g, 2 * p + c, span]
                    side = side_of(g, p, c, t) * inside
                    if TILE * t < halo:
                        mid, side = mid * not_top, side * not_top
                    if TILE * t >= halo + rows:
                        mid, side = mid * not_bottom, side * not_bottom
                    weight[0, z, c, span] = mid
                    weight[0, z, 2 + c, span] = side
                    weight[1, z, c, span] = -mid if c else mid
                    weight[1, z, 2 + c, span] = -side if c else side
        return carried

    lax.fori_loop(0, 2, weigh, 0)
    for copy in observed_loads:
        copy.wait()

    clane = lax.broadcasted_iota(jnp.int32, (CHUNK, LANES), 1)
    at_first = clane == 0
    at_last = clane == LANES - 1
    chunks = range(0, ext, CHUNK)

    def at(r):
        return slice(PAD + r, PAD + r + CHUNK)

    def stencil(u, r):
        sums = []
        higher, lower_rows = slice(PAD + r - 1, PAD + r - 1 + CHUNK), slice(PAD + r + 1, PAD + r + 1 + CHUNK)
        for c in range(2):
            mid, side = u[c, at(r)], u[c + 2, at(r)]
            mid_l, mid_r = pltpu.roll(mid, 1, axis=1), pltpu.roll(mid, LANES - 1, axis=1)
            side_l, side_r = pltpu.roll(side, 1, axis=1), pltpu.roll(side, LANES - 1, axis=1)
            in_mid = jnp.where(at_first, side_l, mid_l) + jnp.where(at_last, side_r, mid_r)
            in_side = jnp.where(at_first, mid_l, side_l) + jnp.where(at_last, mid_r, side_r)
            sums.append(
                (
                    in_mid + (u[c, higher] + u[c, lower_rows]),
                    in_side + (u[c + 2, higher] + u[c + 2, lower_rows]),
                )
            )
        return [sums[0][0], sums[1][0], sums[0][1], sums[1][1]]

    def scaled(g, kind, z, r):
        q = [weight[kind, z, k, r : r + CHUNK] for k in range(4)]
        out = []
        for k in (0, 2):
            out.append(g[k] * q[k] - g[k + 1] * q[k + 1])
            out.append(g[k] * q[k + 1] + g[k + 1] * q[k])
        return out

    def relax(kind, s, z):
        for r in chunks:
            v = scaled([held[k, r : r + CHUNK] for k in range(4)], kind, z, r)
            for k in range(4):
                u0[k, at(r)] = v[k]
        for source, target in ((u0, u1), (u1, u2)):
            for r in chunks:
                sums = stencil(source, r)
                v = scaled([held[k, r : r + CHUNK] + sums[k] for k in range(4)], kind, z, r)
                for k in range(4):
                    target[k, at(r)] = v[k]
                if target is u2 and halo <= r < halo + rows:
                    result[kind, s, z, 0, r - halo : r - halo + CHUNK] = v[0]
                    result[kind, s, z, 1, r - halo : r - halo + CHUNK] = v[1]

    most = pl.ds(TILE, ext - 2 * TILE)

    def wait_carry(kind, s):
        @pl.when(kind != lower)
        def _():
            ref = carry_side.at[kind, s]
            remote(ref, ref, cside_send.at[kind, s], cside_recv.at[kind, s], anyone).wait_recv()
            ref = carry.at[kind, s, :, most]
            remote(ref, ref, carry_send.at[kind, s], carry_recv.at[kind, s], anyone).wait_recv()

    def hand_on(kind, s):
        for c in range(2):
            for t in range(ext // TILE):
                leave[kind, s, c, TILE * t : TILE * t + TILE] = u2[c, PAD + TILE * t : PAD + TILE * t + TILE]
            for_left, for_right = fold(
                lambda j, k: u2[c, PAD + TILE * k : PAD + TILE * k + TILE], 1, ext // TILE
            )
            leave_side[kind, s, 0, c] = for_left
            leave_side[kind, s, 1, c] = for_right

        @pl.when(kind == lower)
        def _():
            for source, device in ((0, through[1]), (1, through[2])):
                remote(
                    leave_side.at[kind, s, source],
                    carry_side.at[kind, s, 1 - source],
                    cside_send.at[kind, s],
                    cside_recv.at[kind, s],
                    device,
                ).start()
            remote(
                leave.at[kind, s, :, most],
                carry.at[kind, s, :, most],
                carry_send.at[kind, s],
                carry_recv.at[kind, s],
                through[0],
            ).start()

    def field_out(s):
        away = result.at[0, s, pl.ds(planes * (1 - half), planes)]
        remote(away, fout.at[:, :, mine + s], out_send.at[s], out_recv.at[s], partner).start()
        here = result.at[0, s, pl.ds(planes * half, planes)]
        pltpu.make_async_copy(here, fout.at[:, :, mine + s], load.at[s]).start()

    def remain(s, carried):
        ref = observed.at[s, 1 - half]
        remote(ref, ref, obs_send.at[s], obs_recv.at[s], anyone).wait_recv()
        for h in (1, 0):
            g = residual_group(s, h)
            for p in range(planes):
                for c in range(2):
                    data[g, 2 * p + c, halo : halo + rows] = (
                        result[0, s, planes * h + p, c] - observed[s, h, 2 * p + c]
                    )
            exchange(g)
        return carried

    def step(i, carried):
        kind, s = i // 2, lax.rem(i, 2)
        for h in range(2):
            arrive(4 * kind + 2 * s + h)

        @pl.when((kind == 1) & (lower == 0))
        def _():
            field_out(s)

        wait_carry(kind, s)
        for t in range(ext // TILE):
            span = slice(TILE * t, TILE * t + TILE)
            where = slice(PAD + TILE * t, PAD + TILE * t + TILE)
            for c in range(2):
                u2[c, where] = carry[kind, s, c, span]
                u2[2 + c, where] = unfold(carry_side[kind, s, 0, c], carry_side[kind, s, 1, c], t)

        def plane(j, inner):
            z = jnp.where(kind == 0, j, 2 * planes - 1 - j)
            h, p = z // planes, lax.rem(z, planes)
            g = 4 * kind + 2 * s + h
            for t in range(ext // TILE):
                span = slice(TILE * t, TILE * t + TILE)
                where = slice(PAD + TILE * t, PAD + TILE * t + TILE)
                for c in range(2):
                    held[c, span] = data[g, 2 * p + c, span] + 2.5 * u2[c, where]
                    held[2 + c, span] = side_of(g, p, c, t) + 2.5 * u2[2 + c, where]
            relax(kind, s, z)

            @pl.when(kind == 1)
            def _():
                value = total[z]
                for c in range(2):
                    value = value + result[0, s, z, c] * result[1, s, z, c]
                total[z] = value

            @pl.when((i == 3) & (h != half))
            def _():
                remote(total.at[z], other.at[p], grad_send.at[p], grad_recv.at[p], partner).start()

            return inner

        lax.fori_loop(0, 2 * planes, plane, 0)
        hand_on(kind, s)

        @pl.when((kind == 1) & (lower == 1))
        def _():
            field_out(s)

        @pl.when(kind == 0)
        def _():
            start = jnp.where(lower == 1, s, 0)
            end = jnp.where(lower == 1, s + 1, 2 * s)
            lax.fori_loop(start, end, remain, 0)

        return carried

    lax.fori_loop(0, 4, step, 0)

    def finish(g, carried):
        remote(edges(g), edges(g), row_send.at[g], row_recv.at[g], anyone).wait_send()
        remote(sides.at[g], sides.at[g], side_send.at[g], side_recv.at[g], anyone).wait_send()
        return carried

    lax.fori_loop(0, 10, finish, 0)
    whole = data.at[0, :, block]
    for k in range(3):
        remote(whole, whole, in_send.at[k], in_recv.at[k], anyone).wait_send()
    for s in range(2):
        ref = observed.at[s, 0]
        remote(ref, ref, obs_send.at[s], obs_recv.at[s], anyone).wait_send()
        ref = result.at[0, s, pl.ds(planes * (1 - half), planes)]
        remote(ref, ref, out_send.at[s], out_recv.at[s], anyone).wait_send()
        remote(ref, ref, out_send.at[s], out_recv.at[s], anyone).wait_recv()
        pltpu.make_async_copy(
            result.at[0, s, pl.ds(planes * half, planes)], fout.at[:, :, mine + s], load.at[s]
        ).wait()
        for kind in range(2):

            @pl.when(kind == lower)
            def _():
                side, main = leave_side.at[kind, s], leave.at[kind, s, :, most]
                remote(side, side, cside_send.at[kind, s], cside_recv.at[kind, s], anyone).wait_send()
                remote(main, main, carry_send.at[kind, s], carry_recv.at[kind, s], anyone).wait_send()

    sent = [remote(other.at[p], other.at[p], grad_send.at[p], grad_recv.at[p], anyone) for p in range(planes)]
    for copy in sent:
        copy.wait_recv()
    held[0:planes, 0:rows] = (total[pl.ds(planes * half, planes)] + other[...]) * (1.0 / shots)
    pltpu.sync_copy(held.at[0:planes, 0:rows], gout)
    for copy in sent:
        copy.wait_send()


def body(sizes, source, observed, wavenumber, damping):
    planes, comps, shots, rows, lanes = source.shape
    ndepth = sizes[0]
    edge = 4 * planes
    halo = 2 * edge
    ext = rows + 2 * halo
    assert comps == 2 and planes == 2 and shots == 4 and ndepth == 4
    assert lanes == LANES and edge * 2 * rows == TILE * LANES
    vmem = lambda *shape: pltpu.VMEM(shape, jnp.float32)
    dma = lambda *shape: pltpu.SemaphoreType.DMA(shape)
    anywhere = pl.BlockSpec(memory_space=pl.ANY)
    return pl.pallas_call(
        functools.partial(kernel, sizes, halo, edge),
        name="sweeps",
        out_shape=(
            jax.ShapeDtypeStruct(source.shape, jnp.float32),
            jax.ShapeDtypeStruct(wavenumber.shape, jnp.float32),
        ),
        in_specs=[anywhere] * 4,
        out_specs=(anywhere, anywhere),
        scratch_shapes=[
            vmem(10, 4, ext, lanes),
            vmem(10, 2, 3, 2, TILE, lanes),
            vmem(10, 2, 2, TILE, lanes),
            vmem(2, 2, 4, rows, lanes),
            vmem(2, 4, 4, ext, lanes),
            vmem(2, 2, 2, ext, lanes),
            vmem(2, 2, 2, 2, TILE, lanes),
            vmem(2, 2, 2, ext, lanes),
            vmem(2, 2, 2, 2, TILE, lanes),
            vmem(2, 2, 4, 2, rows, lanes),
            vmem(4, ext + 2 * PAD, lanes),
            vmem(4, ext + 2 * PAD, lanes),
            vmem(4, ext + 2 * PAD, lanes),
            vmem(4, ext, lanes),
            vmem(4, rows, lanes),
            vmem(2, rows, lanes),
            dma(10),
            dma(10),
            dma(10),
            dma(10),
            dma(10),
            dma(2, 2),
            dma(2, 2),
            dma(2, 2),
            dma(2, 2),
            dma(3),
            dma(3),
            dma(2),
            dma(2),
            dma(2),
            dma(2),
            dma(2),
            dma(2),
        ],
        compiler_params=pltpu.CompilerParams(
            collective_id=0, has_side_effects=True, vmem_limit_bytes=24 << 20
        ),
    )(*(pltpu.with_memory_space_constraint(x, pltpu.HBM) for x in (source, observed, wavenumber, damping)))


def solution(mesh):
    sizes = tuple(mesh.shape[axis] for axis in ("depth", "gx", "gy"))
    return jax.shard_map(
        functools.partial(body, sizes),
        mesh=mesh,
        in_specs=(
            P("depth", None, None, "gx", "gy"),
            P("depth", None, None, "gx", "gy"),
            P("depth", "gx", "gy"),
            P("depth", "gx", "gy"),
        ),
        out_specs=(P("depth", None, None, "gx", "gy"), P("depth", "gx", "gy")),
        check_vma=False,
    )
```

```python
import functools

import jax
import jax.numpy as jnp
from jax import lax
from jax.experimental import pallas as pl
from jax.experimental.pallas import tpu as pltpu
from jax.sharding import PartitionSpec as P

MESH = pl.DeviceIdType.MESH
CHUNK = 16
PAD = 8
LANES = 128
TILE = 8


def kernel(
    sizes,
    halo,
    edge,
    src,
    obs,
    wavenumber,
    damping,
    fout,
    gout,
    data,
    sides,
    folded,
    observed,
    weight,
    carry,
    carry_side,
    leave,
    leave_side,
    result,
    u0,
    u1,
    u2,
    held,
    total,
    other,
    load,
    row_send,
    row_recv,
    side_send,
    side_recv,
    carry_send,
    carry_recv,
    cside_send,
    cside_recv,
    in_send,
    in_recv,
    obs_send,
    obs_recv,
    out_send,
    out_recv,
    grad_send,
    grad_recv,
):
    ndepth, ngx, ngy = sizes
    d = lax.axis_index("depth")
    a = lax.axis_index("gx")
    b = lax.axis_index("gy")
    planes, _, shots, rows, _ = src.shape
    ext = rows + 2 * halo
    block = pl.ds(halo, rows)
    half = lax.rem(d, 2)
    lower = d // 2
    mine = 2 * lax.rem(d + lower, 2)
    theirs = 2 - mine

    def source_group(s, h):
        return 2 * s + h

    def residual_group(s, h):
        return 4 + 2 * s + h

    def inverse_group(h):
        return 8 + h

    up, down = lax.rem(a + ngx - 1, ngx), lax.rem(a + 1, ngx)
    left, right = lax.rem(b + ngy - 1, ngy), lax.rem(b + 1, ngy)
    beside = [
        {"gx": x, "gy": y}
        for x, y in (
            (up, b),
            (down, b),
            (a, left),
            (a, right),
            (up, left),
            (up, right),
            (down, left),
            (down, right),
        )
    ]
    partner = {"depth": d + 1 - 2 * half}
    through = [{"depth": ndepth - 1 - d, "gy": y} for y in (b, left, right)]
    anyone = beside[0]

    barrier = pltpu.get_barrier_semaphore()
    partners = beside + [partner] + through
    for device in partners:
        pl.semaphore_signal(barrier, inc=1, device_id=device, device_id_type=MESH)

    def remote(source, target, send, recv, device):
        return pltpu.make_async_remote_copy(
            src_ref=source,
            dst_ref=target,
            send_sem=send,
            recv_sem=recv,
            device_id=device,
            device_id_type=MESH,
        )

    inverse_loads = [
        pltpu.make_async_copy(wavenumber, held.at[0:planes, 0:rows], load.at[0]),
        pltpu.make_async_copy(damping, held.at[planes : 2 * planes, 0:rows], load.at[1]),
    ]
    source_loads, observed_loads = [], []
    for s in range(2):
        for p in range(planes):
            k = 2 + 4 * s + 2 * p
            pair = pl.ds(2 * p, 2)
            source_loads.append(
                pltpu.make_async_copy(
                    src.at[p, :, mine + s], data.at[source_group(s, half), pair, block], load.at[k]
                )
            )
            observed_loads.append(
                pltpu.make_async_copy(
                    obs.at[p, :, mine + s], observed.at[s, half, pair], load.at[k + 1]
                )
            )
    for copy in inverse_loads + source_loads + observed_loads:
        copy.start()

    for copy in inverse_loads:
        copy.wait()
    for p in range(planes):
        real_diag = 6.0 - held[p, 0:rows]
        damp = held[planes + p, 0:rows]
        denom = real_diag * real_diag + damp * damp
        data[inverse_group(half), 2 * p, halo : halo + rows] = real_diag / denom
        data[inverse_group(half), 2 * p + 1, halo : halo + rows] = -damp / denom

    pl.semaphore_wait(barrier, len(partners))

    own_inverse = data.at[inverse_group(half), :, block]
    remote(own_inverse, own_inverse, in_send.at[0], in_recv.at[0], partner).start()
    for s in range(2):
        for p in range(planes):
            remote(
                src.at[p, :, theirs + s],
                data.at[source_group(s, half), pl.ds(2 * p, 2), block],
                in_send.at[1 + s],
                in_recv.at[1 + s],
                partner,
            ).start()

    for u in (u0, u1):
        u[...] = jnp.zeros_like(u)
    for k in range(4):
        u2[k, 0:PAD] = jnp.zeros_like(u2[k, 0:PAD])
        u2[k, PAD + ext : 2 * PAD + ext] = jnp.zeros_like(u2[k, 0:PAD])
    total[...] = jnp.zeros_like(total)
    none = jnp.zeros((TILE, LANES), jnp.float32)
    for s in range(2):
        for c in range(2):
            for t in range(ext // TILE):
                carry[lower, s, c, TILE * t : TILE * t + TILE] = none
            carry[1 - lower, s, c, 0:TILE] = none
            carry[1 - lower, s, c, ext - TILE : ext] = none
            for side in range(2):
                carry_side[lower, s, side, c] = none

    lane = lax.broadcasted_iota(jnp.int32, (TILE, LANES), 1)
    lane_group = lane // edge
    groups = LANES // edge

    def fold(read, count, tiles):
        for_left = for_right = None
        for k in range(tiles):
            for j in range(count):
                at = k * count + j
                moved = pltpu.roll(read(j, k), (edge * (at + 1)) % LANES, axis=1)
                if for_left is None:
                    for_left = for_right = moved
                else:
                    for_left = jnp.where(lane_group == (at + 1) % groups, moved, for_left)
                    for_right = jnp.where(lane_group == at, moved, for_right)
        return for_left, for_right

    def unfold(from_left, from_right, at):
        shift = (LANES - edge * (at + 1)) % LANES
        return jnp.where(
            lane < LANES // 2,
            pltpu.roll(from_right, shift, axis=1),
            pltpu.roll(from_left, shift, axis=1),
        )

    def exchange(g):
        for device, source, target in (
            (beside[0], pl.ds(halo, halo), pl.ds(halo + rows, halo)),
            (beside[1], pl.ds(rows, halo), pl.ds(0, halo)),
        ):
            remote(
                data.at[g, :, source], data.at[g, :, target], row_send.at[g], row_recv.at[g], device
            ).start()
        for p in range(planes):
            for_left, for_right = fold(
                lambda c, k: data[g, 2 * p + c, halo + TILE * k : halo + TILE * k + TILE], 2, rows // TILE
            )
            folded[g, 0, p] = for_left
            folded[g, 1, p] = for_right
        for device, source, side, piece in (
            (beside[2], 0, 1, 1),
            (beside[3], 1, 0, 1),
            (beside[4], 0, 1, 2),
            (beside[5], 1, 0, 2),
            (beside[6], 0, 1, 0),
            (beside[7], 1, 0, 0),
        ):
            remote(
                folded.at[g, source], sides.at[g, side, piece], side_send.at[g], side_recv.at[g], device
            ).start()

    def edges(g):
        return data.at[g, :, pl.ds(0, 2 * halo)]

    def arrive(g):
        remote(edges(g), edges(g), row_send.at[g], row_recv.at[g], anyone).wait_recv()
        remote(sides.at[g], sides.at[g], side_send.at[g], side_recv.at[g], anyone).wait_recv()

    def side_of(g, p, c, t):
        spare = halo // TILE
        inner = rows // TILE
        if t < spare:
            piece, k = 0, t + inner - spare
        elif t < spare + inner:
            piece, k = 1, t - spare
        else:
            piece, k = 2, t - spare - inner
        return unfold(sides[g, 0, piece, p], sides[g, 1, piece, p], 2 * k + c)

    exchange(inverse_group(half))
    for copy in source_loads:
        copy.wait()

    def landed(k, g):
        whole = data.at[g, :, block]
        remote(whole, whole, in_send.at[k], in_recv.at[k], anyone).wait_recv()
        exchange(g)

    def send_observed():
        for s in range(2):
            for p in range(planes):
                remote(
                    obs.at[p, :, theirs + s],
                    observed.at[s, half, pl.ds(2 * p, 2)],
                    obs_send.at[s],
                    obs_recv.at[s],
                    partner,
                ).start()

    def spread(i, c):
        @pl.when(i < 2)
        def _():
            exchange(source_group(i, half))

        @pl.when(i >= 2)
        def _():
            landed(i - 2, jnp.where(i == 2, inverse_group(1 - half), source_group(i - 3, 1 - half)))

        @pl.when((i == 4) & (lower == 1))
        def _():
            send_observed()

        return c

    lax.fori_loop(0, 5, spread, 0)
    not_top = (a > 0).astype(jnp.float32)
    not_bottom = (a < ngx - 1).astype(jnp.float32)
    not_left = (b > 0).astype(jnp.float32)
    not_right = (b < ngy - 1).astype(jnp.float32)
    inside = jnp.where(lane < edge, not_right, jnp.where(lane >= LANES - edge, not_left, 0.0))

    def weigh(h, carried):
        g = inverse_group(h)
        arrive(g)
        for p in range(planes):
            z = planes * h + p
            for t in range(ext // TILE):
                span = slice(TILE * t, TILE * t + TILE)
                for c in range(2):
                    mid = data[g, 2 * p + c, span]
                    side = side_of(g, p, c, t) * inside
                    if TILE * t < halo:
                        mid, side = mid * not_top, side * not_top
                    if TILE * t >= halo + rows:
                        mid, side = mid * not_bottom, side * not_bottom
                    weight[0, z, c, span] = mid
                    weight[0, z, 2 + c, span] = side
                    weight[1, z, c, span] = -mid if c else mid
                    weight[1, z, 2 + c, span] = -side if c else side
        return carried

    lax.fori_loop(0, 2, weigh, 0)
    for copy in observed_loads:
        copy.wait()

    clane = lax.broadcasted_iota(jnp.int32, (CHUNK, LANES), 1)
    at_first = clane == 0
    at_last = clane == LANES - 1
    chunks = range(0, ext, CHUNK)

    def at(r):
        return slice(PAD + r, PAD + r + CHUNK)

    def stencil(u, r):
        sums = []
        higher, lower_rows = slice(PAD + r - 1, PAD + r - 1 + CHUNK), slice(PAD + r + 1, PAD + r + 1 + CHUNK)
        for c in range(2):
            mid, side = u[c, at(r)], u[c + 2, at(r)]
            mid_l, mid_r = pltpu.roll(mid, 1, axis=1), pltpu.roll(mid, LANES - 1, axis=1)
            side_l, side_r = pltpu.roll(side, 1, axis=1), pltpu.roll(side, LANES - 1, axis=1)
            in_mid = jnp.where(at_first, side_l, mid_l) + jnp.where(at_last, side_r, mid_r)
            in_side = jnp.where(at_first, mid_l, side_l) + jnp.where(at_last, mid_r, side_r)
            sums.append(
                (
                    in_mid + (u[c, higher] + u[c, lower_rows]),
                    in_side + (u[c + 2, higher] + u[c + 2, lower_rows]),
                )
            )
        return [sums[0][0], sums[1][0], sums[0][1], sums[1][1]]

    def scaled(g, kind, z, r):
        q = [weight[kind, z, k, r : r + CHUNK] for k in range(4)]
        out = []
        for k in (0, 2):
            out.append(g[k] * q[k] - g[k + 1] * q[k + 1])
            out.append(g[k] * q[k + 1] + g[k + 1] * q[k])
        return out

    def relax(kind, s, z):
        for r in chunks:
            v = scaled([held[k, r : r + CHUNK] for k in range(4)], kind, z, r)
            for k in range(4):
                u0[k, at(r)] = v[k]
        for source, target in ((u0, u1), (u1, u2)):
            for r in chunks:
                sums = stencil(source, r)
                v = scaled([held[k, r : r + CHUNK] + sums[k] for k in range(4)], kind, z, r)
                for k in range(4):
                    target[k, at(r)] = v[k]
                if target is u2 and halo <= r < halo + rows:
                    result[kind, s, z, 0, r - halo : r - halo + CHUNK] = v[0]
                    result[kind, s, z, 1, r - halo : r - halo + CHUNK] = v[1]

    most = pl.ds(TILE, ext - 2 * TILE)

    def wait_carry(kind, s):
        @pl.when(kind != lower)
        def _():
            ref = carry_side.at[kind, s]
            remote(ref, ref, cside_send.at[kind, s], cside_recv.at[kind, s], anyone).wait_recv()
            ref = carry.at[kind, s, :, most]
            remote(ref, ref, carry_send.at[kind, s], carry_recv.at[kind, s], anyone).wait_recv()

    def hand_on(kind, s):
        for c in range(2):
            for t in range(ext // TILE):
                leave[kind, s, c, TILE * t : TILE * t + TILE] = u2[c, PAD + TILE * t : PAD + TILE * t + TILE]
            for_left, for_right = fold(
                lambda j, k: u2[c, PAD + TILE * k : PAD + TILE * k + TILE], 1, ext // TILE
            )
            leave_side[kind, s, 0, c] = for_left
            leave_side[kind, s, 1, c] = for_right

        @pl.when(kind == lower)
        def _():
            for source, device in ((0, through[1]), (1, through[2])):
                remote(
                    leave_side.at[kind, s, source],
                    carry_side.at[kind, s, 1 - source],
                    cside_send.at[kind, s],
                    cside_recv.at[kind, s],
                    device,
                ).start()
            remote(
                leave.at[kind, s, :, most],
                carry.at[kind, s, :, most],
                carry_send.at[kind, s],
                carry_recv.at[kind, s],
                through[0],
            ).start()

    def field_out(s):
        away = result.at[0, s, pl.ds(planes * (1 - half), planes)]
        remote(away, fout.at[:, :, mine + s], out_send.at[s], out_recv.at[s], partner).start()
        here = result.at[0, s, pl.ds(planes * half, planes)]
        pltpu.make_async_copy(here, fout.at[:, :, mine + s], load.at[s]).start()

    def remain(s, carried):
        ref = observed.at[s, 1 - half]
        remote(ref, ref, obs_send.at[s], obs_recv.at[s], anyone).wait_recv()
        for h in (1, 0):
            g = residual_group(s, h)
            for p in range(planes):
                for c in range(2):
                    data[g, 2 * p + c, halo : halo + rows] = (
                        result[0, s, planes * h + p, c] - observed[s, h, 2 * p + c]
                    )
            exchange(g)
        return carried

    def step(i, carried):
        kind, s = i // 2, lax.rem(i, 2)
        for h in range(2):
            arrive(4 * kind + 2 * s + h)

        wait_carry(kind, s)
        for t in range(ext // TILE):
            span = slice(TILE * t, TILE * t + TILE)
            where = slice(PAD + TILE * t, PAD + TILE * t + TILE)
            for c in range(2):
                u2[c, where] = carry[kind, s, c, span]
                u2[2 + c, where] = unfold(carry_side[kind, s, 0, c], carry_side[kind, s, 1, c], t)

        def plane(j, inner):
            z = jnp.where(kind == 0, j, 2 * planes - 1 - j)
            h, p = z // planes, lax.rem(z, planes)
            g = 4 * kind + 2 * s + h
            for t in range(ext // TILE):
                span = slice(TILE * t, TILE * t + TILE)
                where = slice(PAD + TILE * t, PAD + TILE * t + TILE)
                for c in range(2):
                    held[c, span] = data[g, 2 * p + c, span] + 2.5 * u2[c, where]
                    held[2 + c, span] = side_of(g, p, c, t) + 2.5 * u2[2 + c, where]
            relax(kind, s, z)

            @pl.when(kind == 1)
            def _():
                value = total[z]
                for c in range(2):
                    value = value + result[0, s, z, c] * result[1, s, z, c]
                total[z] = value

            @pl.when((i == 3) & (h != half))
            def _():
                remote(total.at[z], other.at[p], grad_send.at[p], grad_recv.at[p], partner).start()

            return inner

        lax.fori_loop(0, 2 * planes, plane, 0)
        hand_on(kind, s)

        @pl.when((kind == 1) & (lower == 1))
        def _():
            field_out(s)

        @pl.when(kind == 0)
        def _():
            @pl.when((lower == 0) & (s == 1))
            def _():
                send_observed()
                for q in range(2):
                    field_out(q)

            start = jnp.where(lower == 1, s, 0)
            end = jnp.where(lower == 1, s + 1, 2 * s)
            lax.fori_loop(start, end, remain, 0)

        return carried

    lax.fori_loop(0, 4, step, 0)

    def finish(g, carried):
        remote(edges(g), edges(g), row_send.at[g], row_recv.at[g], anyone).wait_send()
        remote(sides.at[g], sides.at[g], side_send.at[g], side_recv.at[g], anyone).wait_send()
        return carried

    lax.fori_loop(0, 10, finish, 0)
    whole = data.at[0, :, block]
    for k in range(3):
        remote(whole, whole, in_send.at[k], in_recv.at[k], anyone).wait_send()
    for s in range(2):
        ref = observed.at[s, 0]
        remote(ref, ref, obs_send.at[s], obs_recv.at[s], anyone).wait_send()
        ref = result.at[0, s, pl.ds(planes * (1 - half), planes)]
        remote(ref, ref, out_send.at[s], out_recv.at[s], anyone).wait_send()
        remote(ref, ref, out_send.at[s], out_recv.at[s], anyone).wait_recv()
        pltpu.make_async_copy(
            result.at[0, s, pl.ds(planes * half, planes)], fout.at[:, :, mine + s], load.at[s]
        ).wait()
        for kind in range(2):

            @pl.when(kind == lower)
            def _():
                side, main = leave_side.at[kind, s], leave.at[kind, s, :, most]
                remote(side, side, cside_send.at[kind, s], cside_recv.at[kind, s], anyone).wait_send()
                remote(main, main, carry_send.at[kind, s], carry_recv.at[kind, s], anyone).wait_send()

    sent = [remote(other.at[p], other.at[p], grad_send.at[p], grad_recv.at[p], anyone) for p in range(planes)]
    for copy in sent:
        copy.wait_recv()
    held[0:planes, 0:rows] = (total[pl.ds(planes * half, planes)] + other[...]) * (1.0 / shots)
    pltpu.sync_copy(held.at[0:planes, 0:rows], gout)
    for copy in sent:
        copy.wait_send()


def body(sizes, source, observed, wavenumber, damping):
    planes, comps, shots, rows, lanes = source.shape
    ndepth = sizes[0]
    edge = 4 * planes
    halo = 2 * edge
    ext = rows + 2 * halo
    assert comps == 2 and planes == 2 and shots == 4 and ndepth == 4
    assert lanes == LANES and edge * 2 * rows == TILE * LANES
    vmem = lambda *shape: pltpu.VMEM(shape, jnp.float32)
    dma = lambda *shape: pltpu.SemaphoreType.DMA(shape)
    anywhere = pl.BlockSpec(memory_space=pl.ANY)
    return pl.pallas_call(
        functools.partial(kernel, sizes, halo, edge),
        name="sweeps",
        out_shape=(
            jax.ShapeDtypeStruct(source.shape, jnp.float32),
            jax.ShapeDtypeStruct(wavenumber.shape, jnp.float32),
        ),
        in_specs=[anywhere] * 4,
        out_specs=(anywhere, anywhere),
        scratch_shapes=[
            vmem(10, 4, ext, lanes),
            vmem(10, 2, 3, 2, TILE, lanes),
            vmem(10, 2, 2, TILE, lanes),
            vmem(2, 2, 4, rows, lanes),
            vmem(2, 4, 4, ext, lanes),
            vmem(2, 2, 2, ext, lanes),
            vmem(2, 2, 2, 2, TILE, lanes),
            vmem(2, 2, 2, ext, lanes),
            vmem(2, 2, 2, 2, TILE, lanes),
            vmem(2, 2, 4, 2, rows, lanes),
            vmem(4, ext + 2 * PAD, lanes),
            vmem(4, ext + 2 * PAD, lanes),
            vmem(4, ext + 2 * PAD, lanes),
            vmem(4, ext, lanes),
            vmem(4, rows, lanes),
            vmem(2, rows, lanes),
            dma(10),
            dma(10),
            dma(10),
            dma(10),
            dma(10),
            dma(2, 2),
            dma(2, 2),
            dma(2, 2),
            dma(2, 2),
            dma(3),
            dma(3),
            dma(2),
            dma(2),
            dma(2),
            dma(2),
            dma(2),
            dma(2),
        ],
        compiler_params=pltpu.CompilerParams(
            collective_id=0, has_side_effects=True, vmem_limit_bytes=24 << 20
        ),
    )(*(pltpu.with_memory_space_constraint(x, pltpu.HBM) for x in (source, observed, wavenumber, damping)))


def solution(mesh):
    sizes = tuple(mesh.shape[axis] for axis in ("depth", "gx", "gy"))
    return jax.shard_map(
        functools.partial(body, sizes),
        mesh=mesh,
        in_specs=(
            P("depth", None, None, "gx", "gy"),
            P("depth", None, None, "gx", "gy"),
            P("depth", "gx", "gy"),
            P("depth", "gx", "gy"),
        ),
        out_specs=(P("depth", None, None, "gx", "gy"), P("depth", "gx", "gy")),
        check_vma=False,
    )
```

```python
import functools

import jax
import jax.numpy as jnp
from jax import lax
from jax.experimental import pallas as pl
from jax.experimental.pallas import tpu as pltpu
from jax.sharding import PartitionSpec as P

MESH = pl.DeviceIdType.MESH
CHUNK = 16
PAD = 8
LANES = 128
TILE = 8


def kernel(
    sizes,
    halo,
    edge,
    src,
    obs,
    wavenumber,
    damping,
    fout,
    gout,
    data,
    sides,
    folded,
    observed,
    weight,
    carry,
    carry_side,
    leave,
    leave_side,
    result,
    u0,
    u1,
    u2,
    held,
    total,
    other,
    load,
    row_send,
    row_recv,
    side_send,
    side_recv,
    carry_send,
    carry_recv,
    cside_send,
    cside_recv,
    in_send,
    in_recv,
    obs_send,
    obs_recv,
    out_send,
    out_recv,
    grad_send,
    grad_recv,
):
    ndepth, ngx, ngy = sizes
    d = lax.axis_index("depth")
    a = lax.axis_index("gx")
    b = lax.axis_index("gy")
    planes, _, shots, rows, _ = src.shape
    ext = rows + 2 * halo
    block = pl.ds(halo, rows)
    half = lax.rem(d, 2)
    lower = d // 2
    mine = 2 * lax.rem(d + lower, 2)
    theirs = 2 - mine

    def source_group(s, h):
        return 2 * s + h

    def residual_group(s, h):
        return 4 + 2 * s + h

    def inverse_group(h):
        return 8 + h

    up, down = lax.rem(a + ngx - 1, ngx), lax.rem(a + 1, ngx)
    left, right = lax.rem(b + ngy - 1, ngy), lax.rem(b + 1, ngy)
    beside = [
        {"gx": x, "gy": y}
        for x, y in (
            (up, b),
            (down, b),
            (a, left),
            (a, right),
            (up, left),
            (up, right),
            (down, left),
            (down, right),
        )
    ]
    partner = {"depth": d + 1 - 2 * half}
    through = [{"depth": ndepth - 1 - d, "gy": y} for y in (b, left, right)]
    anyone = beside[0]

    barrier = pltpu.get_barrier_semaphore()
    partners = beside + [partner] + through
    for device in partners:
        pl.semaphore_signal(barrier, inc=1, device_id=device, device_id_type=MESH)

    def remote(source, target, send, recv, device):
        return pltpu.make_async_remote_copy(
            src_ref=source,
            dst_ref=target,
            send_sem=send,
            recv_sem=recv,
            device_id=device,
            device_id_type=MESH,
        )

    inverse_loads = [
        pltpu.make_async_copy(wavenumber, held.at[0:planes, 0:rows], load.at[0]),
        pltpu.make_async_copy(damping, held.at[planes : 2 * planes, 0:rows], load.at[1]),
    ]
    source_loads, observed_loads = [], []
    for s in range(2):
        for p in range(planes):
            k = 2 + 4 * s + 2 * p
            pair = pl.ds(2 * p, 2)
            source_loads.append(
                pltpu.make_async_copy(
                    src.at[p, :, mine + s], data.at[source_group(s, half), pair, block], load.at[k]
                )
            )
            observed_loads.append(
                pltpu.make_async_copy(
                    obs.at[p, :, mine + s], observed.at[s, half, pair], load.at[k + 1]
                )
            )
    for copy in inverse_loads + source_loads + observed_loads:
        copy.start()

    for copy in inverse_loads:
        copy.wait()
    for p in range(planes):
        real_diag = 6.0 - held[p, 0:rows]
        damp = held[planes + p, 0:rows]
        denom = real_diag * real_diag + damp * damp
        data[inverse_group(half), 2 * p, halo : halo + rows] = real_diag / denom
        data[inverse_group(half), 2 * p + 1, halo : halo + rows] = -damp / denom

    pl.semaphore_wait(barrier, len(partners))

    def send_observed():
        for s in range(2):
            for p in range(planes):
                remote(
                    obs.at[p, :, theirs + s],
                    observed.at[s, half, pl.ds(2 * p, 2)],
                    obs_send.at[s],
                    obs_recv.at[s],
                    partner,
                ).start()

    own_inverse = data.at[inverse_group(half), :, block]
    remote(own_inverse, own_inverse, in_send.at[0], in_recv.at[0], partner).start()
    for s in range(2):
        for p in range(planes):
            remote(
                src.at[p, :, theirs + s],
                data.at[source_group(s, half), pl.ds(2 * p, 2), block],
                in_send.at[1 + s],
                in_recv.at[1 + s],
                partner,
            ).start()

    @pl.when(lower == 1)
    def _():
        send_observed()

    for u in (u0, u1):
        u[...] = jnp.zeros_like(u)
    for k in range(4):
        u2[k, 0:PAD] = jnp.zeros_like(u2[k, 0:PAD])
        u2[k, PAD + ext : 2 * PAD + ext] = jnp.zeros_like(u2[k, 0:PAD])
    total[...] = jnp.zeros_like(total)
    none = jnp.zeros((TILE, LANES), jnp.float32)
    for s in range(2):
        for c in range(2):
            for t in range(ext // TILE):
                carry[lower, s, c, TILE * t : TILE * t + TILE] = none
            carry[1 - lower, s, c, 0:TILE] = none
            carry[1 - lower, s, c, ext - TILE : ext] = none
            for side in range(2):
                carry_side[lower, s, side, c] = none

    lane = lax.broadcasted_iota(jnp.int32, (TILE, LANES), 1)
    lane_group = lane // edge
    groups = LANES // edge

    def fold(read, count, tiles):
        for_left = for_right = None
        for k in range(tiles):
            for j in range(count):
                at = k * count + j
                moved = pltpu.roll(read(j, k), (edge * (at + 1)) % LANES, axis=1)
                if for_left is None:
                    for_left = for_right = moved
                else:
                    for_left = jnp.where(lane_group == (at + 1) % groups, moved, for_left)
                    for_right = jnp.where(lane_group == at, moved, for_right)
        return for_left, for_right

    def unfold(from_left, from_right, at):
        shift = (LANES - edge * (at + 1)) % LANES
        return jnp.where(
            lane < LANES // 2,
            pltpu.roll(from_right, shift, axis=1),
            pltpu.roll(from_left, shift, axis=1),
        )

    def exchange(g):
        for device, source, target in (
            (beside[0], pl.ds(halo, halo), pl.ds(halo + rows, halo)),
            (beside[1], pl.ds(rows, halo), pl.ds(0, halo)),
        ):
            remote(
                data.at[g, :, source], data.at[g, :, target], row_send.at[g], row_recv.at[g], device
            ).start()
        for p in range(planes):
            for_left, for_right = fold(
                lambda c, k: data[g, 2 * p + c, halo + TILE * k : halo + TILE * k + TILE], 2, rows // TILE
            )
            folded[g, 0, p] = for_left
            folded[g, 1, p] = for_right
        for device, source, side, piece in (
            (beside[2], 0, 1, 1),
            (beside[3], 1, 0, 1),
            (beside[4], 0, 1, 2),
            (beside[5], 1, 0, 2),
            (beside[6], 0, 1, 0),
            (beside[7], 1, 0, 0),
        ):
            remote(
                folded.at[g, source], sides.at[g, side, piece], side_send.at[g], side_recv.at[g], device
            ).start()

    def edges(g):
        return data.at[g, :, pl.ds(0, 2 * halo)]

    def arrive(g):
        remote(edges(g), edges(g), row_send.at[g], row_recv.at[g], anyone).wait_recv()
        remote(sides.at[g], sides.at[g], side_send.at[g], side_recv.at[g], anyone).wait_recv()

    def side_of(g, p, c, t):
        spare = halo // TILE
        inner = rows // TILE
        if t < spare:
            piece, k = 0, t + inner - spare
        elif t < spare + inner:
            piece, k = 1, t - spare
        else:
            piece, k = 2, t - spare - inner
        return unfold(sides[g, 0, piece, p], sides[g, 1, piece, p], 2 * k + c)

    exchange(inverse_group(half))
    for copy in source_loads:
        copy.wait()

    def landed(k, g):
        whole = data.at[g, :, block]
        remote(whole, whole, in_send.at[k], in_recv.at[k], anyone).wait_recv()
        exchange(g)

    def spread(i, c):
        @pl.when(i < 2)
        def _():
            exchange(source_group(i, half))

        @pl.when(i >= 2)
        def _():
            landed(i - 2, jnp.where(i == 2, inverse_group(1 - half), source_group(i - 3, 1 - half)))

        return c

    lax.fori_loop(0, 5, spread, 0)
    not_top = (a > 0).astype(jnp.float32)
    not_bottom = (a < ngx - 1).astype(jnp.float32)
    not_left = (b > 0).astype(jnp.float32)
    not_right = (b < ngy - 1).astype(jnp.float32)
    inside = jnp.where(lane < edge, not_right, jnp.where(lane >= LANES - edge, not_left, 0.0))

    def weigh(h, carried):
        g = inverse_group(h)
        arrive(g)
        for p in range(planes):
            z = planes * h + p
            for t in range(ext // TILE):
                span = slice(TILE * t, TILE * t + TILE)
                for c in range(2):
                    mid = data[g, 2 * p + c, span]
                    side = side_of(g, p, c, t) * inside
                    if TILE * t < halo:
                        mid, side = mid * not_top, side * not_top
                    if TILE * t >= halo + rows:
                        mid, side = mid * not_bottom, side * not_bottom
                    weight[0, z, c, span] = mid
                    weight[0, z, 2 + c, span] = side
                    weight[1, z, c, span] = -mid if c else mid
                    weight[1, z, 2 + c, span] = -side if c else side
        return carried

    lax.fori_loop(0, 2, weigh, 0)
    for copy in observed_loads:
        copy.wait()

    clane = lax.broadcasted_iota(jnp.int32, (CHUNK, LANES), 1)
    at_first = clane == 0
    at_last = clane == LANES - 1
    chunks = range(0, ext, CHUNK)

    def at(r):
        return slice(PAD + r, PAD + r + CHUNK)

    def stencil(u, r):
        sums = []
        higher, lower_rows = slice(PAD + r - 1, PAD + r - 1 + CHUNK), slice(PAD + r + 1, PAD + r + 1 + CHUNK)
        for c in range(2):
            mid, side = u[c, at(r)], u[c + 2, at(r)]
            mid_l, mid_r = pltpu.roll(mid, 1, axis=1), pltpu.roll(mid, LANES - 1, axis=1)
            side_l, side_r = pltpu.roll(side, 1, axis=1), pltpu.roll(side, LANES - 1, axis=1)
            in_mid = jnp.where(at_first, side_l, mid_l) + jnp.where(at_last, side_r, mid_r)
            in_side = jnp.where(at_first, mid_l, side_l) + jnp.where(at_last, mid_r, side_r)
            sums.append(
                (
                    in_mid + (u[c, higher] + u[c, lower_rows]),
                    in_side + (u[c + 2, higher] + u[c + 2, lower_rows]),
                )
            )
        return [sums[0][0], sums[1][0], sums[0][1], sums[1][1]]

    def scaled(g, kind, z, r):
        q = [weight[kind, z, k, r : r + CHUNK] for k in range(4)]
        out = []
        for k in (0, 2):
            out.append(g[k] * q[k] - g[k + 1] * q[k + 1])
            out.append(g[k] * q[k + 1] + g[k + 1] * q[k])
        return out

    def relax(kind, s, z):
        for r in chunks:
            v = scaled([held[k, r : r + CHUNK] for k in range(4)], kind, z, r)
            for k in range(4):
                u0[k, at(r)] = v[k]
        for source, target in ((u0, u1), (u1, u2)):
            for r in chunks:
                sums = stencil(source, r)
                v = scaled([held[k, r : r + CHUNK] + sums[k] for k in range(4)], kind, z, r)
                for k in range(4):
                    target[k, at(r)] = v[k]
                if target is u2 and halo <= r < halo + rows:
                    result[kind, s, z, 0, r - halo : r - halo + CHUNK] = v[0]
                    result[kind, s, z, 1, r - halo : r - halo + CHUNK] = v[1]

    most = pl.ds(TILE, ext - 2 * TILE)

    def wait_carry(kind, s):
        @pl.when(kind != lower)
        def _():
            ref = carry_side.at[kind, s]
            remote(ref, ref, cside_send.at[kind, s], cside_recv.at[kind, s], anyone).wait_recv()
            ref = carry.at[kind, s, :, most]
            remote(ref, ref, carry_send.at[kind, s], carry_recv.at[kind, s], anyone).wait_recv()

    def hand_on(kind, s):
        for c in range(2):
            for t in range(ext // TILE):
                leave[kind, s, c, TILE * t : TILE * t + TILE] = u2[c, PAD + TILE * t : PAD + TILE * t + TILE]
            for_left, for_right = fold(
                lambda j, k: u2[c, PAD + TILE * k : PAD + TILE * k + TILE], 1, ext // TILE
            )
            leave_side[kind, s, 0, c] = for_left
            leave_side[kind, s, 1, c] = for_right

        @pl.when(kind == lower)
        def _():
            for source, device in ((0, through[1]), (1, through[2])):
                remote(
                    leave_side.at[kind, s, source],
                    carry_side.at[kind, s, 1 - source],
                    cside_send.at[kind, s],
                    cside_recv.at[kind, s],
                    device,
                ).start()
            remote(
                leave.at[kind, s, :, most],
                carry.at[kind, s, :, most],
                carry_send.at[kind, s],
                carry_recv.at[kind, s],
                through[0],
            ).start()

    def field_out(s):
        away = result.at[0, s, pl.ds(planes * (1 - half), planes)]
        remote(away, fout.at[:, :, mine + s], out_send.at[s], out_recv.at[s], partner).start()
        here = result.at[0, s, pl.ds(planes * half, planes)]
        pltpu.make_async_copy(here, fout.at[:, :, mine + s], load.at[s]).start()

    def remain(s, carried):
        ref = observed.at[s, 1 - half]
        remote(ref, ref, obs_send.at[s], obs_recv.at[s], anyone).wait_recv()
        for h in (1, 0):
            g = residual_group(s, h)
            for p in range(planes):
                for c in range(2):
                    data[g, 2 * p + c, halo : halo + rows] = (
                        result[0, s, planes * h + p, c] - observed[s, h, 2 * p + c]
                    )
            exchange(g)
        return carried

    def step(i, carried):
        kind, s = i // 2, lax.rem(i, 2)
        for h in range(2):
            arrive(4 * kind + 2 * s + h)

        wait_carry(kind, s)
        for t in range(ext // TILE):
            span = slice(TILE * t, TILE * t + TILE)
            where = slice(PAD + TILE * t, PAD + TILE * t + TILE)
            for c in range(2):
                u2[c, where] = carry[kind, s, c, span]
                u2[2 + c, where] = unfold(carry_side[kind, s, 0, c], carry_side[kind, s, 1, c], t)

        def plane(j, inner):
            z = jnp.where(kind == 0, j, 2 * planes - 1 - j)
            h, p = z // planes, lax.rem(z, planes)
            g = 4 * kind + 2 * s + h
            for t in range(ext // TILE):
                span = slice(TILE * t, TILE * t + TILE)
                where = slice(PAD + TILE * t, PAD + TILE * t + TILE)
                for c in range(2):
                    held[c, span] = data[g, 2 * p + c, span] + 2.5 * u2[c, where]
                    held[2 + c, span] = side_of(g, p, c, t) + 2.5 * u2[2 + c, where]
            relax(kind, s, z)

            @pl.when(kind == 1)
            def _():
                value = total[z]
                for c in range(2):
                    value = value + result[0, s, z, c] * result[1, s, z, c]
                total[z] = value

            @pl.when((i == 3) & (h != half))
            def _():
                remote(total.at[z], other.at[p], grad_send.at[p], grad_recv.at[p], partner).start()

            return inner

        lax.fori_loop(0, 2 * planes, plane, 0)
        hand_on(kind, s)

        @pl.when((kind == 1) & (lower == 1))
        def _():
            field_out(s)

        @pl.when(kind == 0)
        def _():
            @pl.when((lower == 0) & (s == 1))
            def _():
                send_observed()
                for q in range(2):
                    field_out(q)

            start = jnp.where(lower == 1, s, 0)
            end = jnp.where(lower == 1, s + 1, 2 * s)
            lax.fori_loop(start, end, remain, 0)

        return carried

    lax.fori_loop(0, 4, step, 0)

    def finish(g, carried):
        remote(edges(g), edges(g), row_send.at[g], row_recv.at[g], anyone).wait_send()
        remote(sides.at[g], sides.at[g], side_send.at[g], side_recv.at[g], anyone).wait_send()
        return carried

    lax.fori_loop(0, 10, finish, 0)
    whole = data.at[0, :, block]
    for k in range(3):
        remote(whole, whole, in_send.at[k], in_recv.at[k], anyone).wait_send()
    for s in range(2):
        ref = observed.at[s, 0]
        remote(ref, ref, obs_send.at[s], obs_recv.at[s], anyone).wait_send()
        ref = result.at[0, s, pl.ds(planes * (1 - half), planes)]
        remote(ref, ref, out_send.at[s], out_recv.at[s], anyone).wait_send()
        remote(ref, ref, out_send.at[s], out_recv.at[s], anyone).wait_recv()
        pltpu.make_async_copy(
            result.at[0, s, pl.ds(planes * half, planes)], fout.at[:, :, mine + s], load.at[s]
        ).wait()
        for kind in range(2):

            @pl.when(kind == lower)
            def _():
                side, main = leave_side.at[kind, s], leave.at[kind, s, :, most]
                remote(side, side, cside_send.at[kind, s], cside_recv.at[kind, s], anyone).wait_send()
                remote(main, main, carry_send.at[kind, s], carry_recv.at[kind, s], anyone).wait_send()

    sent = [remote(other.at[p], other.at[p], grad_send.at[p], grad_recv.at[p], anyone) for p in range(planes)]
    for copy in sent:
        copy.wait_recv()
    held[0:planes, 0:rows] = (total[pl.ds(planes * half, planes)] + other[...]) * (1.0 / shots)
    pltpu.sync_copy(held.at[0:planes, 0:rows], gout)
    for copy in sent:
        copy.wait_send()


def body(sizes, source, observed, wavenumber, damping):
    planes, comps, shots, rows, lanes = source.shape
    ndepth = sizes[0]
    edge = 4 * planes
    halo = 2 * edge
    ext = rows + 2 * halo
    assert comps == 2 and planes == 2 and shots == 4 and ndepth == 4
    assert lanes == LANES and edge * 2 * rows == TILE * LANES
    vmem = lambda *shape: pltpu.VMEM(shape, jnp.float32)
    dma = lambda *shape: pltpu.SemaphoreType.DMA(shape)
    anywhere = pl.BlockSpec(memory_space=pl.ANY)
    return pl.pallas_call(
        functools.partial(kernel, sizes, halo, edge),
        name="sweeps",
        out_shape=(
            jax.ShapeDtypeStruct(source.shape, jnp.float32),
            jax.ShapeDtypeStruct(wavenumber.shape, jnp.float32),
        ),
        in_specs=[anywhere] * 4,
        out_specs=(anywhere, anywhere),
        scratch_shapes=[
            vmem(10, 4, ext, lanes),
            vmem(10, 2, 3, 2, TILE, lanes),
            vmem(10, 2, 2, TILE, lanes),
            vmem(2, 2, 4, rows, lanes),
            vmem(2, 4, 4, ext, lanes),
            vmem(2, 2, 2, ext, lanes),
            vmem(2, 2, 2, 2, TILE, lanes),
            vmem(2, 2, 2, ext, lanes),
            vmem(2, 2, 2, 2, TILE, lanes),
            vmem(2, 2, 4, 2, rows, lanes),
            vmem(4, ext + 2 * PAD, lanes),
            vmem(4, ext + 2 * PAD, lanes),
            vmem(4, ext + 2 * PAD, lanes),
            vmem(4, ext, lanes),
            vmem(4, rows, lanes),
            vmem(2, rows, lanes),
            dma(10),
            dma(10),
            dma(10),
            dma(10),
            dma(10),
            dma(2, 2),
            dma(2, 2),
            dma(2, 2),
            dma(2, 2),
            dma(3),
            dma(3),
            dma(2),
            dma(2),
            dma(2),
            dma(2),
            dma(2),
            dma(2),
        ],
        compiler_params=pltpu.CompilerParams(
            collective_id=0, has_side_effects=True, vmem_limit_bytes=24 << 20
        ),
    )(*(pltpu.with_memory_space_constraint(x, pltpu.HBM) for x in (source, observed, wavenumber, damping)))


def solution(mesh):
    sizes = tuple(mesh.shape[axis] for axis in ("depth", "gx", "gy"))
    return jax.shard_map(
        functools.partial(body, sizes),
        mesh=mesh,
        in_specs=(
            P("depth", None, None, "gx", "gy"),
            P("depth", None, None, "gx", "gy"),
            P("depth", "gx", "gy"),
            P("depth", "gx", "gy"),
        ),
        out_specs=(P("depth", None, None, "gx", "gy"), P("depth", "gx", "gy")),
        check_vma=False,
    )
```

```python
import functools

import jax
import jax.numpy as jnp
from jax import lax
from jax.experimental import pallas as pl
from jax.experimental.pallas import tpu as pltpu
from jax.sharding import PartitionSpec as P

MESH = pl.DeviceIdType.MESH
CHUNK = 16
PAD = 8
LANES = 128
TILE = 8


def kernel(
    sizes,
    halo,
    edge,
    src,
    obs,
    wavenumber,
    damping,
    fout,
    gout,
    data,
    sides,
    folded,
    observed,
    weight,
    carry,
    carry_side,
    leave,
    leave_side,
    result,
    u0,
    u1,
    u2,
    held,
    total,
    other,
    load,
    row_send,
    row_recv,
    side_send,
    side_recv,
    carry_send,
    carry_recv,
    cside_send,
    cside_recv,
    in_send,
    in_recv,
    obs_send,
    obs_recv,
    out_send,
    out_recv,
    grad_send,
    grad_recv,
):
    ndepth, ngx, ngy = sizes
    d = lax.axis_index("depth")
    a = lax.axis_index("gx")
    b = lax.axis_index("gy")
    planes, _, shots, rows, _ = src.shape
    ext = rows + 2 * halo
    block = pl.ds(halo, rows)
    half = lax.rem(d, 2)
    lower = d // 2
    mine = 2 * lax.rem(d + lower, 2)
    theirs = 2 - mine

    def source_group(s, h):
        return 2 * s + h

    def residual_group(s, h):
        return 4 + 2 * s + h

    def inverse_group(h):
        return 8 + h

    up, down = lax.rem(a + ngx - 1, ngx), lax.rem(a + 1, ngx)
    left, right = lax.rem(b + ngy - 1, ngy), lax.rem(b + 1, ngy)
    beside = [
        {"gx": x, "gy": y}
        for x, y in (
            (up, b),
            (down, b),
            (a, left),
            (a, right),
            (up, left),
            (up, right),
            (down, left),
            (down, right),
        )
    ]
    partner = {"depth": d + 1 - 2 * half}
    through = [{"depth": ndepth - 1 - d, "gy": y} for y in (b, left, right)]
    anyone = beside[0]

    barrier = pltpu.get_barrier_semaphore()
    partners = beside + [partner] + through
    for device in partners:
        pl.semaphore_signal(barrier, inc=1, device_id=device, device_id_type=MESH)

    def remote(source, target, send, recv, device):
        return pltpu.make_async_remote_copy(
            src_ref=source,
            dst_ref=target,
            send_sem=send,
            recv_sem=recv,
            device_id=device,
            device_id_type=MESH,
        )

    inverse_loads = [
        pltpu.make_async_copy(wavenumber, held.at[0:planes, 0:rows], load.at[0]),
        pltpu.make_async_copy(damping, held.at[planes : 2 * planes, 0:rows], load.at[1]),
    ]
    source_loads, observed_loads = [], []
    for s in range(2):
        for p in range(planes):
            k = 2 + 4 * s + 2 * p
            pair = pl.ds(2 * p, 2)
            source_loads.append(
                pltpu.make_async_copy(
                    src.at[p, :, mine + s], data.at[source_group(s, half), pair, block], load.at[k]
                )
            )
            observed_loads.append(
                pltpu.make_async_copy(
                    obs.at[p, :, mine + s], observed.at[s, half, pair], load.at[k + 1]
                )
            )
    for copy in inverse_loads + source_loads + observed_loads:
        copy.start()

    for copy in inverse_loads:
        copy.wait()
    for p in range(planes):
        real_diag = 6.0 - held[p, 0:rows]
        damp = held[planes + p, 0:rows]
        denom = real_diag * real_diag + damp * damp
        data[inverse_group(half), 2 * p, halo : halo + rows] = real_diag / denom
        data[inverse_group(half), 2 * p + 1, halo : halo + rows] = -damp / denom

    pl.semaphore_wait(barrier, len(partners))

    def send_observed():
        for s in range(2):
            for p in range(planes):
                remote(
                    obs.at[p, :, theirs + s],
                    observed.at[s, half, pl.ds(2 * p, 2)],
                    obs_send.at[s],
                    obs_recv.at[s],
                    partner,
                ).start()

    own_inverse = data.at[inverse_group(half), :, block]
    remote(own_inverse, own_inverse, in_send.at[0], in_recv.at[0], partner).start()
    for s in range(2):
        for p in range(planes):
            remote(
                src.at[p, :, theirs + s],
                data.at[source_group(s, half), pl.ds(2 * p, 2), block],
                in_send.at[1 + s],
                in_recv.at[1 + s],
                partner,
            ).start()

    @pl.when(lower == 1)
    def _():
        send_observed()

    for u in (u0, u1):
        u[...] = jnp.zeros_like(u)
    for k in range(4):
        u2[k, 0:PAD] = jnp.zeros_like(u2[k, 0:PAD])
        u2[k, PAD + ext : 2 * PAD + ext] = jnp.zeros_like(u2[k, 0:PAD])
    total[...] = jnp.zeros_like(total)
    none = jnp.zeros((TILE, LANES), jnp.float32)
    for s in range(2):
        for c in range(2):
            for t in range(ext // TILE):
                carry[lower, s, c, TILE * t : TILE * t + TILE] = none
            carry[1 - lower, s, c, 0:TILE] = none
            carry[1 - lower, s, c, ext - TILE : ext] = none
            for side in range(2):
                carry_side[lower, s, side, c] = none

    lane = lax.broadcasted_iota(jnp.int32, (TILE, LANES), 1)
    lane_group = lane // edge
    groups = LANES // edge

    def fold(read, count, tiles):
        for_left = for_right = None
        for k in range(tiles):
            for j in range(count):
                at = k * count + j
                moved = pltpu.roll(read(j, k), (edge * (at + 1)) % LANES, axis=1)
                if for_left is None:
                    for_left = for_right = moved
                else:
                    for_left = jnp.where(lane_group == (at + 1) % groups, moved, for_left)
                    for_right = jnp.where(lane_group == at, moved, for_right)
        return for_left, for_right

    def unfold(from_left, from_right, at):
        shift = (LANES - edge * (at + 1)) % LANES
        return jnp.where(
            lane < LANES // 2,
            pltpu.roll(from_right, shift, axis=1),
            pltpu.roll(from_left, shift, axis=1),
        )

    def exchange(g):
        for device, source, target in (
            (beside[0], pl.ds(halo, halo), pl.ds(halo + rows, halo)),
            (beside[1], pl.ds(rows, halo), pl.ds(0, halo)),
        ):
            remote(
                data.at[g, :, source], data.at[g, :, target], row_send.at[g], row_recv.at[g], device
            ).start()
        for p in range(planes):
            for_left, for_right = fold(
                lambda c, k: data[g, 2 * p + c, halo + TILE * k : halo + TILE * k + TILE], 2, rows // TILE
            )
            folded[g, 0, p] = for_left
            folded[g, 1, p] = for_right
        for device, source, side, piece in (
            (beside[2], 0, 1, 1),
            (beside[3], 1, 0, 1),
            (beside[4], 0, 1, 2),
            (beside[5], 1, 0, 2),
            (beside[6], 0, 1, 0),
            (beside[7], 1, 0, 0),
        ):
            remote(
                folded.at[g, source], sides.at[g, side, piece], side_send.at[g], side_recv.at[g], device
            ).start()

    def edges(g):
        return data.at[g, :, pl.ds(0, 2 * halo)]

    def arrive(g):
        remote(edges(g), edges(g), row_send.at[g], row_recv.at[g], anyone).wait_recv()
        remote(sides.at[g], sides.at[g], side_send.at[g], side_recv.at[g], anyone).wait_recv()

    def side_of(g, p, c, t):
        spare = halo // TILE
        inner = rows // TILE
        if t < spare:
            piece, k = 0, t + inner - spare
        elif t < spare + inner:
            piece, k = 1, t - spare
        else:
            piece, k = 2, t - spare - inner
        return unfold(sides[g, 0, piece, p], sides[g, 1, piece, p], 2 * k + c)

    exchange(inverse_group(half))
    for copy in source_loads:
        copy.wait()

    def landed(k, g):
        whole = data.at[g, :, block]
        remote(whole, whole, in_send.at[k], in_recv.at[k], anyone).wait_recv()
        exchange(g)

    def spread(i, c):
        @pl.when(i < 2)
        def _():
            exchange(source_group(i, half))

        @pl.when(i >= 2)
        def _():
            landed(i - 2, jnp.where(i == 2, inverse_group(1 - half), source_group(i - 3, 1 - half)))

        return c

    lax.fori_loop(0, 5, spread, 0)
    not_top = (a > 0).astype(jnp.float32)
    not_bottom = (a < ngx - 1).astype(jnp.float32)
    not_left = (b > 0).astype(jnp.float32)
    not_right = (b < ngy - 1).astype(jnp.float32)
    inside = jnp.where(lane < edge, not_right, jnp.where(lane >= LANES - edge, not_left, 0.0))

    def weigh(h, carried):
        g = inverse_group(h)
        arrive(g)
        for p in range(planes):
            z = planes * h + p
            for t in range(ext // TILE):
                span = slice(TILE * t, TILE * t + TILE)
                for c in range(2):
                    mid = data[g, 2 * p + c, span]
                    side = side_of(g, p, c, t) * inside
                    if TILE * t < halo:
                        mid, side = mid * not_top, side * not_top
                    if TILE * t >= halo + rows:
                        mid, side = mid * not_bottom, side * not_bottom
                    weight[0, z, c, span] = mid
                    weight[0, z, 2 + c, span] = side
                    weight[1, z, c, span] = -mid if c else mid
                    weight[1, z, 2 + c, span] = -side if c else side
        return carried

    lax.fori_loop(0, 2, weigh, 0)
    for copy in observed_loads:
        copy.wait()

    clane = lax.broadcasted_iota(jnp.int32, (CHUNK, LANES), 1)
    at_first = clane == 0
    at_last = clane == LANES - 1
    chunks = range(0, ext, CHUNK)

    def at(r):
        return slice(PAD + r, PAD + r + CHUNK)

    def stencil(u, r):
        sums = []
        higher, lower_rows = slice(PAD + r - 1, PAD + r - 1 + CHUNK), slice(PAD + r + 1, PAD + r + 1 + CHUNK)
        for c in range(2):
            mid, side = u[c, at(r)], u[c + 2, at(r)]
            mid_l, mid_r = pltpu.roll(mid, 1, axis=1), pltpu.roll(mid, LANES - 1, axis=1)
            side_l, side_r = pltpu.roll(side, 1, axis=1), pltpu.roll(side, LANES - 1, axis=1)
            in_mid = jnp.where(at_first, side_l, mid_l) + jnp.where(at_last, side_r, mid_r)
            in_side = jnp.where(at_first, mid_l, side_l) + jnp.where(at_last, mid_r, side_r)
            sums.append(
                (
                    in_mid + (u[c, higher] + u[c, lower_rows]),
                    in_side + (u[c + 2, higher] + u[c + 2, lower_rows]),
                )
            )
        return [sums[0][0], sums[1][0], sums[0][1], sums[1][1]]

    def scaled(g, kind, z, r):
        q = [weight[kind, z, k, r : r + CHUNK] for k in range(4)]
        out = []
        for k in (0, 2):
            out.append(g[k] * q[k] - g[k + 1] * q[k + 1])
            out.append(g[k] * q[k + 1] + g[k + 1] * q[k])
        return out

    def relax(kind, s, z):
        for r in chunks:
            v = scaled([held[k, r : r + CHUNK] for k in range(4)], kind, z, r)
            for k in range(4):
                u0[k, at(r)] = v[k]
        for source, target in ((u0, u1), (u1, u2)):
            for r in chunks:
                sums = stencil(source, r)
                v = scaled([held[k, r : r + CHUNK] + sums[k] for k in range(4)], kind, z, r)
                for k in range(4):
                    target[k, at(r)] = v[k]
                if target is u2 and halo <= r < halo + rows:
                    result[kind, s, z, 0, r - halo : r - halo + CHUNK] = v[0]
                    result[kind, s, z, 1, r - halo : r - halo + CHUNK] = v[1]

    most = pl.ds(TILE, ext - 2 * TILE)

    def wait_carry(kind, s):
        @pl.when(kind != lower)
        def _():
            ref = carry_side.at[kind, s]
            remote(ref, ref, cside_send.at[kind, s], cside_recv.at[kind, s], anyone).wait_recv()
            ref = carry.at[kind, s, :, most]
            remote(ref, ref, carry_send.at[kind, s], carry_recv.at[kind, s], anyone).wait_recv()

    def hand_on(kind, s):
        for c in range(2):
            for t in range(ext // TILE):
                leave[kind, s, c, TILE * t : TILE * t + TILE] = u2[c, PAD + TILE * t : PAD + TILE * t + TILE]
            for_left, for_right = fold(
                lambda j, k: u2[c, PAD + TILE * k : PAD + TILE * k + TILE], 1, ext // TILE
            )
            leave_side[kind, s, 0, c] = for_left
            leave_side[kind, s, 1, c] = for_right

        @pl.when(kind == lower)
        def _():
            for source, device in ((0, through[1]), (1, through[2])):
                remote(
                    leave_side.at[kind, s, source],
                    carry_side.at[kind, s, 1 - source],
                    cside_send.at[kind, s],
                    cside_recv.at[kind, s],
                    device,
                ).start()
            for c in range(2):
                remote(
                    leave.at[kind, s, c, most],
                    carry.at[kind, s, c, most],
                    carry_send.at[kind, s],
                    carry_recv.at[kind, s],
                    through[0],
                ).start()

    def field_out(s):
        away = result.at[0, s, pl.ds(planes * (1 - half), planes)]
        remote(away, fout.at[:, :, mine + s], out_send.at[s], out_recv.at[s], partner).start()
        here = result.at[0, s, pl.ds(planes * half, planes)]
        pltpu.make_async_copy(here, fout.at[:, :, mine + s], load.at[s]).start()

    def remain(s, carried):
        ref = observed.at[s, 1 - half]
        remote(ref, ref, obs_send.at[s], obs_recv.at[s], anyone).wait_recv()
        for h in (1, 0):
            g = residual_group(s, h)
            for p in range(planes):
                for c in range(2):
                    data[g, 2 * p + c, halo : halo + rows] = (
                        result[0, s, planes * h + p, c] - observed[s, h, 2 * p + c]
                    )
            exchange(g)
        return carried

    def step(i, carried):
        kind, s = i // 2, lax.rem(i, 2)
        for h in range(2):
            arrive(4 * kind + 2 * s + h)

        wait_carry(kind, s)
        for t in range(ext // TILE):
            span = slice(TILE * t, TILE * t + TILE)
            where = slice(PAD + TILE * t, PAD + TILE * t + TILE)
            for c in range(2):
                u2[c, where] = carry[kind, s, c, span]
                u2[2 + c, where] = unfold(carry_side[kind, s, 0, c], carry_side[kind, s, 1, c], t)

        def plane(j, inner):
            z = jnp.where(kind == 0, j, 2 * planes - 1 - j)
            h, p = z // planes, lax.rem(z, planes)
            g = 4 * kind + 2 * s + h
            for t in range(ext // TILE):
                span = slice(TILE * t, TILE * t + TILE)
                where = slice(PAD + TILE * t, PAD + TILE * t + TILE)
                for c in range(2):
                    held[c, span] = data[g, 2 * p + c, span] + 2.5 * u2[c, where]
                    held[2 + c, span] = side_of(g, p, c, t) + 2.5 * u2[2 + c, where]
            relax(kind, s, z)

            @pl.when(kind == 1)
            def _():
                value = total[z]
                for c in range(2):
                    value = value + result[0, s, z, c] * result[1, s, z, c]
                total[z] = value

            @pl.when((i == 3) & (h != half))
            def _():
                remote(total.at[z], other.at[p], grad_send.at[p], grad_recv.at[p], partner).start()

            return inner

        lax.fori_loop(0, 2 * planes, plane, 0)
        hand_on(kind, s)

        @pl.when((kind == 1) & (lower == 1))
        def _():
            field_out(s)

        @pl.when(kind == 0)
        def _():
            @pl.when((lower == 0) & (s == 1))
            def _():
                send_observed()
                for q in range(2):
                    field_out(q)

            start = jnp.where(lower == 1, s, 0)
            end = jnp.where(lower == 1, s + 1, 2 * s)
            lax.fori_loop(start, end, remain, 0)

        return carried

    lax.fori_loop(0, 4, step, 0)

    def finish(g, carried):
        remote(edges(g), edges(g), row_send.at[g], row_recv.at[g], anyone).wait_send()
        remote(sides.at[g], sides.at[g], side_send.at[g], side_recv.at[g], anyone).wait_send()
        return carried

    lax.fori_loop(0, 10, finish, 0)
    whole = data.at[0, :, block]
    for k in range(3):
        remote(whole, whole, in_send.at[k], in_recv.at[k], anyone).wait_send()
    for s in range(2):
        ref = observed.at[s, 0]
        remote(ref, ref, obs_send.at[s], obs_recv.at[s], anyone).wait_send()
        ref = result.at[0, s, pl.ds(planes * (1 - half), planes)]
        remote(ref, ref, out_send.at[s], out_recv.at[s], anyone).wait_send()
        remote(ref, ref, out_send.at[s], out_recv.at[s], anyone).wait_recv()
        pltpu.make_async_copy(
            result.at[0, s, pl.ds(planes * half, planes)], fout.at[:, :, mine + s], load.at[s]
        ).wait()
        for kind in range(2):

            @pl.when(kind == lower)
            def _():
                side, main = leave_side.at[kind, s], leave.at[kind, s, :, most]
                remote(side, side, cside_send.at[kind, s], cside_recv.at[kind, s], anyone).wait_send()
                remote(main, main, carry_send.at[kind, s], carry_recv.at[kind, s], anyone).wait_send()

    sent = [remote(other.at[p], other.at[p], grad_send.at[p], grad_recv.at[p], anyone) for p in range(planes)]
    for copy in sent:
        copy.wait_recv()
    held[0:planes, 0:rows] = (total[pl.ds(planes * half, planes)] + other[...]) * (1.0 / shots)
    pltpu.sync_copy(held.at[0:planes, 0:rows], gout)
    for copy in sent:
        copy.wait_send()


def body(sizes, source, observed, wavenumber, damping):
    planes, comps, shots, rows, lanes = source.shape
    ndepth = sizes[0]
    edge = 4 * planes
    halo = 2 * edge
    ext = rows + 2 * halo
    assert comps == 2 and planes == 2 and shots == 4 and ndepth == 4
    assert lanes == LANES and edge * 2 * rows == TILE * LANES
    vmem = lambda *shape: pltpu.VMEM(shape, jnp.float32)
    dma = lambda *shape: pltpu.SemaphoreType.DMA(shape)
    anywhere = pl.BlockSpec(memory_space=pl.ANY)
    return pl.pallas_call(
        functools.partial(kernel, sizes, halo, edge),
        name="sweeps",
        out_shape=(
            jax.ShapeDtypeStruct(source.shape, jnp.float32),
            jax.ShapeDtypeStruct(wavenumber.shape, jnp.float32),
        ),
        in_specs=[anywhere] * 4,
        out_specs=(anywhere, anywhere),
        scratch_shapes=[
            vmem(10, 4, ext, lanes),
            vmem(10, 2, 3, 2, TILE, lanes),
            vmem(10, 2, 2, TILE, lanes),
            vmem(2, 2, 4, rows, lanes),
            vmem(2, 4, 4, ext, lanes),
            vmem(2, 2, 2, ext, lanes),
            vmem(2, 2, 2, 2, TILE, lanes),
            vmem(2, 2, 2, ext, lanes),
            vmem(2, 2, 2, 2, TILE, lanes),
            vmem(2, 2, 4, 2, rows, lanes),
            vmem(4, ext + 2 * PAD, lanes),
            vmem(4, ext + 2 * PAD, lanes),
            vmem(4, ext + 2 * PAD, lanes),
            vmem(4, ext, lanes),
            vmem(4, rows, lanes),
            vmem(2, rows, lanes),
            dma(10),
            dma(10),
            dma(10),
            dma(10),
            dma(10),
            dma(2, 2),
            dma(2, 2),
            dma(2, 2),
            dma(2, 2),
            dma(3),
            dma(3),
            dma(2),
            dma(2),
            dma(2),
            dma(2),
            dma(2),
            dma(2),
        ],
        compiler_params=pltpu.CompilerParams(
            collective_id=0, has_side_effects=True, vmem_limit_bytes=24 << 20
        ),
    )(*(pltpu.with_memory_space_constraint(x, pltpu.HBM) for x in (source, observed, wavenumber, damping)))


def solution(mesh):
    sizes = tuple(mesh.shape[axis] for axis in ("depth", "gx", "gy"))
    return jax.shard_map(
        functools.partial(body, sizes),
        mesh=mesh,
        in_specs=(
            P("depth", None, None, "gx", "gy"),
            P("depth", None, None, "gx", "gy"),
            P("depth", "gx", "gy"),
            P("depth", "gx", "gy"),
        ),
        out_specs=(P("depth", None, None, "gx", "gy"), P("depth", "gx", "gy")),
        check_vma=False,
    )
```
